128 devices in a mesh: feat: 8 (over x, z_lo), seq: 16 (over z_hi, y, core).
Axes of the slice: x: 4, y: 4, z: 4 (z_hi: 2, z_lo: 2; z = z_hi * 2 + z_lo), core: 2. Of those that a mesh axis runs over, the one named last changes fastest.
Arguments:
- tokens: bfloat16 [8192, 8192], P('seq', 'feat'), may hold values from -6 to 6
- block_weights: bfloat16 [28672, 512], P('feat'), may hold values from -0.25 to 0.25
- left_factor: bfloat16 [28672, 256], P('feat'), may hold values from -0.09375 to 0.09375
- right_factor: bfloat16 [8192, 256], P('feat'), may hold values from -0.0625 to 0.0625
- pattern: int32 [224, 4], P('feat'), may hold values from 0 to 63, as said below
- cotangent: bfloat16 [8192, 28672], P('seq', 'feat'), may hold values from -6 to 6
Outputs:
- activated: bfloat16 [8192, 28672], P('seq', 'feat')
- grad_input: bfloat16 [16, 512, 8192], P('seq', 'feat')
- grad_blocks: float32 [28672, 512], P(('feat', 'seq'))
- grad_left: float32 [28672, 256], P(('feat', 'seq'))
- grad_right: float32 [8192, 256], P(('feat', 'seq'))
The draws below stay inside these ranges and needn't reach their ends.
Inputs may be any that keep to these rules, and one draw needn't show every extreme that they name: For block row f, pattern[f, 0] // 8 equals (f * 8) // 224, and pattern[f, j] = pattern[f, 0] XOR ((64) >> j) for 1 <= j < 4.
All inputs are finite; a program needn't handle non-finite values.
Results may differ from the reference program's by a relative error of at most 0.0051.
Values may be sent and summed in bfloat16 or wider, within the bound.
A program may use at most 192 MiB of HBM per device.

```python
import jax
import jax.numpy as jnp
from jax import lax

D = 8192
FF = 28672
R = 256
BLK = 128
LEVELS = 4
TOK_DEV = 512
TOKENS = 8192
N_SEQ = 16


def draw_pattern(key, part):
    row_count = FF // BLK
    col_count = D // BLK
    group_width = col_count // 8
    row_ids = jnp.arange(row_count, dtype=jnp.int32)
    offsets = jax.random.randint(key, (row_count,), 0, group_width, dtype=jnp.int32)
    first_col = row_ids * 8 // row_count * group_width + offsets
    columns = [first_col] + [jnp.bitwise_xor(first_col, col_count >> level) for level in range(1, LEVELS)]
    return jnp.stack(columns, axis=1).astype(jnp.int32)


def spiked(drawn, own_key, source, target, blocks, factor):
    def block_of(position):
        return (jnp.arange(drawn.shape[position]) // (drawn.shape[position] // blocks)).reshape((-1,) + (1,) * (drawn.ndim - 1 - position))

    near = jax.random.permutation(own_key, blocks)[block_of(target)]
    other_side = (block_of(target) + blocks // 2) % blocks
    return jnp.where((block_of(source) == near) | (block_of(source) == other_side), factor * drawn, drawn)


def block_levels(key, extent, cuts, least, largest):
    level, own = 1.0, jax.random.fold_in(key, 6)
    for dim, parts in cuts:
        steps = jnp.exp(jax.random.uniform(jax.random.fold_in(own, dim), (parts,), jnp.float32, least / len(cuts), largest / len(cuts)))
        level = level * jnp.repeat(steps, extent[dim] // parts).reshape([-1 if axis == dim else 1 for axis in range(len(extent))])
    return level


def bell_draw(key, dims, scale, most, shards=(), held_as=jnp.bfloat16):
    drawn = scale * jax.random.normal(key, dims, jnp.float32)
    if shards:
        drawn = drawn * block_levels(key, dims, shards, -0.22, 0.18)
    return jnp.clip(drawn, -most, most).astype(held_as)


def gaussian_with(stream_key, shape, scale, limit, pieces, heavy, kind=jnp.bfloat16):
    entries = scale * jax.random.normal(stream_key, shape, jnp.float32)
    if pieces:
        entries = entries * block_levels(stream_key, shape, pieces, -0.22, 0.18)
    return jnp.clip(spiked(entries, jax.random.fold_in(stream_key, 3), *heavy), -limit, limit).astype(kind)


def setup_inputs(seed: int = 0) -> dict:
    key_of = jax.random.split(jax.random.key(seed), 7)
    tokens = gaussian_with(key_of[0], (TOKENS, D), 1.0, 6.0, ((0, 16), (1, 8)), (0, 1, 16, 2.0))
    block_weights = bell_draw(key_of[1], (FF, LEVELS * BLK), (LEVELS * BLK) ** -0.5, 0.25, ((0, 8),))
    left_factor = bell_draw(key_of[2], (FF, R), (16 * R) ** -0.5, 0.09375, ((0, 8),))
    right_factor = bell_draw(key_of[3], (D, R), D ** -0.5, 0.0625, ((0, 8),))
    pattern = draw_pattern(jax.random.fold_in(key_of[6], 71), 0)
    cotangent = gaussian_with(key_of[5], (TOKENS, FF), 1.0, 6.0, ((0, 16), (1, 8)), (0, 1, 16, 2.0))
    return dict(tokens=tokens, block_weights=block_weights, left_factor=left_factor, right_factor=right_factor, pattern=pattern, cotangent=cotangent)


def activation(values):
    return jax.nn.gelu(values, approximate=True)

def reference(tokens, block_weights, left_factor, right_factor, pattern, cotangent):
    row_blocks = FF // BLK
    col_blocks = D // BLK
    weight_blocks = block_weights.astype(jnp.float32).reshape(row_blocks, BLK, LEVELS, BLK)
    left_wide = left_factor.astype(jnp.float32)
    right_wide = right_factor.astype(jnp.float32)
    tok_blocks = tokens.reshape(N_SEQ, TOK_DEV, D)
    cot_blocks = cotangent.reshape(N_SEQ, TOK_DEV, FF)

    def one_block(carry, inputs):
        sum_blocks, sum_left, sum_right = carry
        tok_block, cot_block = inputs
        picked = tok_block.reshape(TOK_DEV, col_blocks, BLK)[:, pattern, :].astype(jnp.float32)
        sparse = jnp.einsum('tfli,foli->tfo', picked, weight_blocks).reshape(TOK_DEV, FF)
        latent = jnp.dot(tok_block, right_factor, preferred_element_type=jnp.float32).astype(jnp.bfloat16)
        latent_wide = latent.astype(jnp.float32)
        pre = sparse + jnp.einsum('tr,or->to', latent_wide, left_wide)
        activated, slope = jax.vjp(activation, pre)
        grad_pre = slope(cot_block.astype(jnp.float32))[0].astype(jnp.bfloat16)
        grad_wide = grad_pre.astype(jnp.float32)
        back_latent = jnp.einsum('to,or->tr', grad_wide, left_wide).astype(jnp.bfloat16)
        back_wide = back_latent.astype(jnp.float32)
        spread = jnp.einsum('tfo,foli->tfli', grad_wide.reshape(TOK_DEV, row_blocks, BLK), weight_blocks)
        input_sparse = jnp.zeros((TOK_DEV, col_blocks, BLK), jnp.float32).at[:, pattern, :].add(spread)
        input_sum = input_sparse.reshape(TOK_DEV, D) + jnp.einsum('tr,ir->ti', back_wide, right_wide)
        block_term = jnp.einsum('tfo,tfli->foli', grad_wide.reshape(TOK_DEV, row_blocks, BLK), picked)
        sum_blocks = sum_blocks + block_term.reshape(FF, LEVELS * BLK)
        sum_left = sum_left + jnp.einsum('to,tr->or', grad_wide, latent_wide)
        sum_right = sum_right + jnp.einsum('ti,tr->ir', tok_block.astype(jnp.float32), back_wide)
        return ((sum_blocks, sum_left, sum_right), (activated.astype(jnp.bfloat16), input_sum.astype(jnp.bfloat16)))
    start_carry = (jnp.zeros((FF, LEVELS * BLK), jnp.float32), jnp.zeros((FF, R), jnp.float32), jnp.zeros((D, R), jnp.float32))
    sums, outputs = lax.scan(one_block, start_carry, (tok_blocks, cot_blocks))
    norm_scale = TOKENS ** (-0.5)
    activated = outputs[0].reshape(TOKENS, FF)
    grad_input = outputs[1]
    return (activated, grad_input, sums[0] * norm_scale, sums[1] * norm_scale, sums[2] * norm_scale)
```

```python
import functools
import math

import jax
import jax.numpy as jnp
from jax import lax
from jax.experimental import pallas as pl
from jax.experimental.pallas import tpu as pltpu
from jax.sharding import PartitionSpec as P

BLK = 128
LEVELS = 4
MESH = pl.DeviceIdType.MESH
F32 = jnp.float32
BF16 = jnp.bfloat16
VMEM_LIMIT = 60 * 1024 * 1024
CHUNKS = 8


def remote(src, dst, send_sem, recv_sem, feat, seq):
    return pltpu.make_async_remote_copy(
        src_ref=src,
        dst_ref=dst,
        send_sem=send_sem,
        recv_sem=recv_sem,
        device_id=(feat, seq),
        device_id_type=MESH,
    )


def feat_neighbours(p):
    x, z = p // 2, p % 2
    flipped = x + 1 - 2 * (x % 2)
    return 2 * flipped + z, 2 * (3 - x) + z, 2 * x + 1 - z


def greet(devices):
    barrier = pltpu.get_barrier_semaphore()
    for feat, seq in devices:
        pl.semaphore_signal(barrier, inc=1, device_id=(feat, seq), device_id_type=MESH)
    pl.semaphore_wait(barrier, len(devices))


def sum_over_feat(p, s, part, landed, shared, rs_send, rs_recv, ag_send, ag_recv):
    count = part.shape[0]
    rs = [
        remote(part.at[(p + k) % count], landed.at[k - 1], rs_send.at[k - 1], rs_recv.at[k - 1], (p + k) % count, s)
        for k in range(1, count)
    ]
    ag = [
        remote(shared.at[p], shared.at[p], ag_send.at[k - 1], ag_recv.at[k - 1], (p + k) % count, s)
        for k in range(1, count)
    ]

    def send():
        for copy in rs:
            copy.start()

    def share():
        total = part[p]
        for k, copy in enumerate(rs):
            copy.wait_recv()
            total = total + landed[k]
        shared[p] = total.astype(shared.dtype)
        for copy in ag:
            copy.start()

    def finish():
        for copy in ag:
            copy.wait_recv()

    def drain():
        for copy in rs + ag:
            copy.wait_send()

    return send, share, finish, drain


def exchange_kernel(
    tok, right, x1, x2, x3, lat, tokv, part, landed, shared,
    load_sem, x_send, x_recv, f_send, f_recv, z_send, z_recv, rs_send, rs_recv, ag_send, ag_recv,
):
    p, s = lax.axis_index("feat"), lax.axis_index("seq")
    side, back, up = feat_neighbours(p)
    feats, slab = part.shape[0], part.shape[1]
    rows = tok.shape[0] // CHUNKS
    load = pltpu.make_async_copy(tok, tokv, load_sem)
    load.start()
    greet([((p + k) % feats, s) for k in range(1, feats)])

    def at(ref, c):
        return ref.at[pl.ds(c * rows, rows), :]

    own = [remote(at(tok, c), at(x2, c), x_send.at[c], x_recv.at[c], side, s) for c in range(CHUNKS)]
    passed = [remote(at(x2, c), at(x1, c), f_send.at[c], f_recv.at[c], back, s) for c in range(CHUNKS)]
    across = [remote(at(tok, c), at(x3, c), z_send.at[c], z_recv.at[c], up, s) for c in range(CHUNKS)]
    send, share, finish, drain = sum_over_feat(p, s, part, landed, shared, rs_send, rs_recv, ag_send, ag_recv)
    own[0].start()
    across[0].start()
    load.wait()
    for q in range(feats):
        part[q] = jnp.dot(tokv[q * slab : (q + 1) * slab, :], right[...], preferred_element_type=F32)
    send()
    for c in range(1, CHUNKS):
        own[c].start()
        across[c].start()
    for c in range(CHUNKS):
        own[c].wait_recv()
        passed[c].start()
        if c == 3:
            share()
    finish()
    for q in range(feats):
        lat[q * slab : (q + 1) * slab, :] = shared[q]
    for c in range(CHUNKS):
        across[c].wait()
        own[c].wait_send()
        passed[c].wait()
    drain()


def exchange(tokens, right):
    rows, width = tokens.shape
    rank = right.shape[1]
    feats = lax.axis_size("feat")
    slab = rows // feats
    whole = jax.ShapeDtypeStruct((rows, width), BF16)
    any_spec = pl.BlockSpec(memory_space=pl.ANY)
    vmem_spec = pl.BlockSpec(memory_space=pltpu.VMEM)
    dma = pltpu.SemaphoreType.DMA
    return pl.pallas_call(
        exchange_kernel,
        out_shape=(whole, whole, whole, jax.ShapeDtypeStruct((rows, rank), BF16)),
        in_specs=[any_spec, vmem_spec],
        out_specs=(any_spec, any_spec, any_spec, vmem_spec),
        scratch_shapes=[
            pltpu.VMEM((rows, width), BF16),
            pltpu.VMEM((feats, slab, rank), F32),
            pltpu.VMEM((feats - 1, slab, rank), F32),
            pltpu.VMEM((feats, slab, rank), BF16),
            dma,
            dma((CHUNKS,)), dma((CHUNKS,)), dma((CHUNKS,)), dma((CHUNKS,)), dma((CHUNKS,)), dma((CHUNKS,)),
            dma((feats - 1,)), dma((feats - 1,)), dma((feats - 1,)), dma((feats - 1,)),
        ],
        compiler_params=pltpu.CompilerParams(collective_id=0, has_side_effects=True, vmem_limit_bytes=VMEM_LIMIT),
    )(tokens, right)


def rows_kernel(norm_scale, lid_ref, tok, x1, x2, x3, lat, w, left, cot, act, terms, back, grads, acc):
    f = pl.program_id(0)

    @pl.when(f == 0)
    def _():
        acc[...] = jnp.zeros_like(acc)
        back[...] = jnp.zeros_like(back)

    lid = lid_ref[f]
    col = pl.ds(pl.multiple_of(lid * BLK, BLK), BLK)
    xl = jnp.concatenate([tok[:, col], x1[:, col], x2[:, col], x3[:, col], lat[...]], axis=1)
    wl = jnp.concatenate([w[...], left[...]], axis=1)
    pre = lax.dot_general(xl, wl, (((1,), (1,)), ((), ())), preferred_element_type=F32)
    c = math.sqrt(2.0 / math.pi)
    square = pre * pre
    th = jnp.tanh(c * (pre + 0.044715 * (square * pre)))
    half = 0.5 + 0.5 * th
    act[...] = (pre * half).astype(BF16)
    slope = half + (0.5 * c) * pre * (1.0 - th * th) * (1.0 + (3.0 * 0.044715) * square)
    gp = (cot[...].astype(F32) * slope).astype(BF16)
    spread = jnp.dot(gp, wl, preferred_element_type=F32)
    wide = LEVELS * BLK
    acc[lid] += spread[:, :wide]
    back[...] += spread[:, wide:]
    grads[...] = (
        lax.dot_general(gp, xl, (((0,), (0,)), ((), ())), preferred_element_type=F32) * norm_scale
    ).astype(BF16)

    @pl.when(f == pl.num_programs(0) - 1)
    def _():
        for j in range(LEVELS):
            for b in range(acc.shape[0]):
                terms[j, :, b * BLK : (b + 1) * BLK] = acc[b, :, j * BLK : (j + 1) * BLK].astype(BF16)


def block_rows(lids, tokens, x1, x2, x3, latent, weights, left, cotangent, norm_scale):
    rows, width = tokens.shape
    out_rows, wide = weights.shape
    rank = left.shape[1]
    whole = pl.BlockSpec((rows, width), lambda f, lid: (0, 0))
    return pl.pallas_call(
        functools.partial(rows_kernel, norm_scale),
        grid_spec=pltpu.PrefetchScalarGridSpec(
            num_scalar_prefetch=1,
            grid=(out_rows // BLK,),
            in_specs=[
                whole, whole, whole, whole,
                pl.BlockSpec((rows, rank), lambda f, lid: (0, 0)),
                pl.BlockSpec((BLK, wide), lambda f, lid: (f, 0)),
                pl.BlockSpec((BLK, rank), lambda f, lid: (f, 0)),
                pl.BlockSpec((rows, BLK), lambda f, lid: (0, f)),
            ],
            out_specs=[
                pl.BlockSpec((rows, BLK), lambda f, lid: (0, f)),
                pl.BlockSpec((LEVELS, rows, width), lambda f, lid: (0, 0, 0)),
                pl.BlockSpec((rows, rank), lambda f, lid: (0, 0)),
                pl.BlockSpec((BLK, wide + rank), lambda f, lid: (f, 0)),
            ],
            scratch_shapes=[pltpu.VMEM((width // BLK, rows, wide), F32)],
        ),
        out_shape=(
            jax.ShapeDtypeStruct((rows, out_rows), BF16),
            jax.ShapeDtypeStruct((LEVELS, rows, width), BF16),
            jax.ShapeDtypeStruct((rows, rank), F32),
            jax.ShapeDtypeStruct((out_rows, wide + rank), BF16),
        ),
        compiler_params=pltpu.CompilerParams(vmem_limit_bytes=VMEM_LIMIT),
    )(lids, tokens, x1, x2, x3, latent, weights, left, cotangent)


def gather_kernel(
    norm_scale, terms, part, right, tok, grads, gin, gblocks, gleft, gright,
    landed, shared, backv, low, rx1, mid, rx2, rz, fin, a2a,
    crecv, q, ry2, ry1, zsend, zrecv, grsend, grrecv,
    rs_send, rs_recv, ag_send, ag_recv, x1s, x1r, x2s, x2r, zs, zr, as_, ar,
    cs, cr, y2s, y2r, y1s, y1r, hs, hr, gs, gr,
):
    p, s = lax.axis_index("feat"), lax.axis_index("seq")
    side, back, up = feat_neighbours(p)
    feats, slab = part.shape[0], part.shape[1]
    seqs = 16
    core, y, half = s % 2, (s // 2) % 4, s // 8
    piece = gblocks.shape[0]
    wide = gblocks.shape[1]

    def seq_at(half_, y_, core_):
        return half_ * 8 + y_ * 2 + core_

    greet(
        [((p + k) % feats, s) for k in range(1, feats)] + [(p, (s + k) % seqs) for k in range(1, seqs)]
    )
    send, share, finish, drain = sum_over_feat(p, s, part, landed, shared, rs_send, rs_recv, ag_send, ag_recv)
    send()

    def at(ref, c):
        return ref.at[pl.ds(c * slab, slab), :]

    first = [remote(at(terms.at[1], c), at(rx1, c), x1s.at[c], x1r.at[c], back, s) for c in range(feats)]
    second = [remote(at(mid, c), at(rx2, c), x2s.at[c], x2r.at[c], side, s) for c in range(feats)]
    across = [remote(at(terms.at[3], c), at(rz, c), zs.at[c], zr.at[c], up, s) for c in range(feats)]
    for c in range(feats):
        first[c].start()
        across[c].start()

    slots = [(dy, h) for dy in (2, 1, 3, 0) for h in (0, 1)]

    def rows_of(dy, h, core_):
        there = half if h == 1 else 1 - half
        return pl.ds(pl.multiple_of(seq_at(there, (y + dy) % 4, core_) * piece, 32), piece)

    sibling = seq_at(half, y, 1 - core)
    up_y, down_y = seq_at(half, (y + 1) % 4, core), seq_at(half, (y + 3) % 4, core)
    other_half = seq_at(1 - half, y, core)
    cores = [
        remote(grads.at[rows_of(dy, h, 1 - core), :], crecv.at[i], cs.at[i], cr.at[i], p, sibling)
        for i, (dy, h) in enumerate(slots)
    ]
    for copy in cores:
        copy.start()
    far = [
        remote(q.at[0], ry2.at[0], y2s.at[0], y2r.at[0], p, up_y),
        remote(q.at[1], ry2.at[1], y2s.at[1], y2r.at[1], p, down_y),
    ]
    near = [remote(q.at[2 + i], ry1.at[i], y1s.at[i], y1r.at[i], p, up_y if i < 2 else down_y) for i in range(4)]

    def pair_sum(i):
        dy, h = slots[i]
        cores[i].wait_recv()
        q[i] = (grads[rows_of(dy, h, core), :].astype(F32) + crecv[i].astype(F32)).astype(BF16)

    share()
    for i in range(2):
        pair_sum(i)
        far[i].start()
    for i in range(2, 6):
        pair_sum(i)
    near[1].start()
    near[2].start()
    finish()
    for c in range(feats):
        backv[c * slab : (c + 1) * slab, :] = shared[c]
    product = lax.dot_general(tok[...], backv[...], (((0,), (0,)), ((), ())), preferred_element_type=F32) * norm_scale
    grow = gright.shape[0]
    for k in range(seqs):
        grsend[k] = product[k * grow : (k + 1) * grow, :].astype(BF16)
    rights = [
        remote(grsend.at[(s + k) % seqs], grrecv.at[k - 1], gs.at[k - 1], gr.at[k - 1], p, (s + k) % seqs)
        for k in range(1, seqs)
    ]
    for copy in rights:
        copy.start()

    def relay(c):
        first[c].wait_recv()
        here = slice(c * slab, (c + 1) * slab)
        mid[here, :] = (terms[2, here, :].astype(F32) + rx1[here, :].astype(F32)).astype(BF16)
        second[c].start()

    for c in range(4):
        relay(c)
    far[0].wait_recv()
    q[2] = (q[2].astype(F32) + ry2[0].astype(F32)).astype(BF16)
    near[0].start()
    far[1].wait_recv()
    q[5] = (q[5].astype(F32) + ry2[1].astype(F32)).astype(BF16)
    near[3].start()
    for i in range(6, 8):
        pair_sum(i)
    for c in range(4, feats):
        relay(c)
    low[...] = lax.dot_general(backv[...], right[...], (((1,), (1,)), ((), ())), preferred_element_type=F32)
    for c in range(feats):
        here = slice(c * slab, (c + 1) * slab)
        second[c].wait_recv()
        across[c].wait_recv()
        fin[c] = (
            low[here, :]
            + terms[0, here, :].astype(F32)
            + rx2[here, :].astype(F32)
            + rz[here, :].astype(F32)
        ).astype(BF16)
    spread = [
        remote(fin.at[(p + k) % feats], a2a.at[p], as_.at[k - 1], ar.at[k - 1], (p + k) % feats, s)
        for k in range(1, feats)
    ]
    for copy in spread:
        copy.start()
    a2a[p] = fin[p]
    for copy in near:
        copy.wait_recv()
    zsend[...] = (q[6].astype(F32) + ry1[0].astype(F32) + ry1[2].astype(F32)).astype(BF16)
    cross = remote(zsend, zrecv, hs, hr, p, other_half)
    cross.start()
    total = grsend[s].astype(F32)
    for k, copy in enumerate(rights):
        copy.wait_recv()
        total = total + grrecv[k].astype(F32)
    gright[...] = total
    for copy in spread:
        copy.wait_recv()
    for c in range(feats):
        gin[:, c * a2a.shape[2] : (c + 1) * a2a.shape[2]] = a2a[c]
    cross.wait_recv()
    mine = q[7].astype(F32) + ry1[1].astype(F32) + ry1[3].astype(F32) + zrecv[...].astype(F32)
    gblocks[...] = mine[:, :wide]
    gleft[...] = mine[:, wide:]
    drain()
    for copy in first + second + across + cores + far + near + rights + spread + [cross]:
        copy.wait_send()


def gather(terms, part, right, tokens, grads, norm_scale):
    rows, width = tokens.shape
    rank = right.shape[1]
    feats, seqs = lax.axis_size("feat"), lax.axis_size("seq")
    slab = rows // feats
    out_rows, wide_all = grads.shape
    piece = out_rows // seqs
    grow = width // seqs
    vmem_spec = pl.BlockSpec(memory_space=pltpu.VMEM)
    dma = pltpu.SemaphoreType.DMA
    f1, s1 = dma((feats - 1,)), dma((seqs - 1,))
    return pl.pallas_call(
        functools.partial(gather_kernel, norm_scale),
        out_shape=(
            jax.ShapeDtypeStruct((slab, feats * width), BF16),
            jax.ShapeDtypeStruct((piece, wide_all - rank), F32),
            jax.ShapeDtypeStruct((piece, rank), F32),
            jax.ShapeDtypeStruct((grow, rank), F32),
        ),
        in_specs=[vmem_spec] * 5,
        out_specs=(vmem_spec,) * 4,
        scratch_shapes=[
            pltpu.VMEM((feats - 1, slab, rank), F32),
            pltpu.VMEM((feats, slab, rank), BF16),
            pltpu.VMEM((rows, rank), BF16),
            pltpu.VMEM((rows, width), F32),
            pltpu.VMEM((rows, width), BF16),
            pltpu.VMEM((rows, width), BF16),
            pltpu.VMEM((rows, width), BF16),
            pltpu.VMEM((rows, width), BF16),
            pltpu.VMEM((feats, slab, width), BF16),
            pltpu.VMEM((feats, slab, width), BF16),
            pltpu.VMEM((8, piece, wide_all), BF16),
            pltpu.VMEM((8, piece, wide_all), BF16),
            pltpu.VMEM((2, piece, wide_all), BF16),
            pltpu.VMEM((4, piece, wide_all), BF16),
            pltpu.VMEM((piece, wide_all), BF16),
            pltpu.VMEM((piece, wide_all), BF16),
            pltpu.VMEM((seqs, grow, rank), BF16),
            pltpu.VMEM((seqs - 1, grow, rank), BF16),
            f1, f1, f1, f1,
            dma((feats,)), dma((feats,)), dma((feats,)), dma((feats,)), dma((feats,)), dma((feats,)), f1, f1,
            dma((8,)), dma((8,)), dma((2,)), dma((2,)), dma((4,)), dma((4,)), dma, dma, s1, s1,
        ],
        compiler_params=pltpu.CompilerParams(collective_id=1, has_side_effects=True, vmem_limit_bytes=VMEM_LIMIT),
    )(terms, part.reshape(feats, slab, rank), right, tokens, grads)


def local(tokens, block_weights, left_factor, right_factor, pattern, cotangent):
    tok_rows, local_width = tokens.shape
    norm_scale = 1.0 / math.sqrt(tok_rows * lax.axis_size("seq"))
    lids = pattern[:, 0] % (local_width // BLK)
    x1, x2, x3, latent = exchange(tokens, right_factor)
    activated, terms, back_part, grads = block_rows(
        lids, tokens, x1, x2, x3, latent, block_weights, left_factor, cotangent, norm_scale
    )
    grad_input, grad_blocks, grad_left, grad_right = gather(
        terms, back_part, right_factor, tokens, grads, norm_scale
    )
    return activated, grad_input[None], grad_blocks, grad_left, grad_right


def solution(mesh):
    in_specs = (
        P("seq", "feat"),
        P("feat", None),
        P("feat", None),
        P("feat", None),
        P("feat", None),
        P("seq", "feat"),
    )
    out_specs = (
        P("seq", "feat"),
        P("seq", "feat", None),
        P(("feat", "seq"), None),
        P(("feat", "seq"), None),
        P(("feat", "seq"), None),
    )
    return jax.shard_map(local, mesh=mesh, in_specs=in_specs, out_specs=out_specs, check_vma=False)
```

```python
import functools
import math

import jax
import jax.numpy as jnp
from jax import lax
from jax.experimental import pallas as pl
from jax.experimental.pallas import tpu as pltpu
from jax.sharding import PartitionSpec as P

BLK = 128
LEVELS = 4
FEATS = 8
SEQS = 16
UNROLL = 4
MESH = pl.DeviceIdType.MESH
F32 = jnp.float32
BF16 = jnp.bfloat16
VMEM_LIMIT = 67043328


def remote(src, dst, send_sem, recv_sem, feat, seq):
    return pltpu.make_async_remote_copy(
        src_ref=src,
        dst_ref=dst,
        send_sem=send_sem,
        recv_sem=recv_sem,
        device_id=(feat, seq),
        device_id_type=MESH,
    )


def greet(devices):
    barrier = pltpu.get_barrier_semaphore()
    for feat, seq in devices:
        pl.semaphore_signal(barrier, inc=1, device_id=(feat, seq), device_id_type=MESH)
    pl.semaphore_wait(barrier, len(devices))


class FeatSum:
    def __init__(self, p, s, part, outgoing, landed, shared, sems):
        rs_send, rs_recv, ag_send, ag_recv = sems
        self.p, self.part, self.outgoing, self.landed, self.shared = p, part, outgoing, landed, shared
        self.rs, self.ag = [], []
        for k in range(1, FEATS):
            there = (p + k) % FEATS
            self.rs.append(
                remote(outgoing.at[there], landed.at[k - 1], rs_send.at[k - 1], rs_recv.at[k - 1], there, s)
            )
            self.ag.append(remote(shared.at[p], shared.at[p], ag_send.at[k - 1], ag_recv.at[k - 1], there, s))

    def send(self):
        self.outgoing[...] = self.part[...].astype(BF16)
        for copy in self.rs:
            copy.start()

    def share(self):
        total = self.part[self.p]
        for k, copy in enumerate(self.rs):
            copy.wait_recv()
            total = total + self.landed[k].astype(F32)
        self.shared[self.p] = total.astype(BF16)
        for copy in self.ag:
            copy.start()

    def finish(self):
        for copy in self.ag:
            copy.wait_recv()

    def drain(self):
        for copy in self.rs + self.ag:
            copy.wait_send()


def loop(first, count, fn):
    def body(i, carry):
        for u in range(UNROLL):
            fn(first + i * UNROLL + u)
        return carry

    lax.fori_loop(0, count // UNROLL, body, 0)
    for u in range(count % UNROLL):
        fn(first + count - count % UNROLL + u)


def block_of(f):
    start = f * BLK
    return pl.ds(start if isinstance(start, int) else pl.multiple_of(start, BLK), BLK)


def kernel(norm_scale, *refs):
    (links, tok, w_hbm, left_hbm, cot_hbm, right) = refs[:6]
    (act_hbm, a2a, grad, gright) = refs[6:10]
    (
        xall, tokv, x1a, x1b, x2a, x2b, x3a, x3b, wv, leftv, gp, actv, sums, terms, grads,
        part, outgoing, landed, shared, lat, landed2, shared2, backv, rx1, rx2, rz,
        crecv, q, ry2, ry1, zsend, zrecv, grsend, grrecv,
    ) = refs[10:44]
    (
        lsem, x_send, x_recv, f_send, f_recv, z_send, z_recv, rs_send, rs_recv, ag_send, ag_recv,
        rs_send2, rs_recv2, ag_send2, ag_recv2, x1s, x1r, x2s, x2r, zs, zr, as_, ar,
        cs, cr, y2s, y2r, y1s, y1r, hs, hr, gs, gr, act_sem,
    ) = refs[44:]
    p, s = lax.axis_index("feat"), lax.axis_index("seq")
    x, z = p // 2, p % 2
    side, back, up = 2 * (x + 1 - 2 * (x % 2)) + z, 2 * (3 - x) + z, 2 * x + 1 - z
    core, y, half = s % 2, (s // 2) % 4, s // 8
    slab, rank = part.shape[1], part.shape[2]
    rows, width = tokv.shape
    mid_rows = rows // 2
    blocks = width // BLK
    row_blocks = wv.shape[0] // BLK
    wide = LEVELS * BLK
    piece = q.shape[1]

    loads = [
        pltpu.make_async_copy(src, dst, lsem.at[i])
        for i, (src, dst) in enumerate([(tok, tokv), (w_hbm, wv), (left_hbm, leftv), (cot_hbm, gp)])
    ]
    for copy in loads:
        copy.start()
    greet([((p + k) % FEATS, s) for k in range(1, FEATS)] + [(p, (s + k) % SEQS) for k in range(1, SEQS)])

    def chunk(pair, c):
        return pair[c // 4].at[pl.ds((c % 4) * slab, slab), :]

    def at(ref, c):
        return ref.at[pl.ds(c * slab, slab), :]

    own = [remote(at(tok, c), chunk((x2a, x2b), c), x_send.at[c], x_recv.at[c], side, s) for c in range(FEATS)]
    passed = [
        remote(chunk((x2a, x2b), c), chunk((x1a, x1b), c), f_send.at[c], f_recv.at[c], back, s) for c in range(FEATS)
    ]
    across = [remote(at(tok, c), chunk((x3a, x3b), c), z_send.at[c], z_recv.at[c], up, s) for c in range(FEATS)]
    latent = FeatSum(p, s, part, outgoing, landed, shared, (rs_send, rs_recv, ag_send, ag_recv))
    own[0].start()
    across[0].start()
    loads[0].wait()
    for c in range(FEATS):
        part[c] = jnp.dot(tokv[c * slab : (c + 1) * slab, :], right[...], preferred_element_type=F32)
    latent.send()
    for c in (1, 2):
        own[c].start()
        across[c].start()

    sums[row_blocks] = jnp.zeros(sums.shape[1:], F32)

    def relay(c):
        own[c].wait_recv()
        passed[c].start()
        if c + 3 < FEATS:
            own[c + 3].start()
            across[c + 3].start()

    relay(0)
    latent.share()
    for c in range(1, 5):
        relay(c)

    def halves(h):
        return slice(h * mid_rows, (h + 1) * mid_rows)

    def repack(h):
        for j, source in enumerate((tokv.at[halves(h), :], (x1a, x1b)[h], (x2a, x2b)[h], (x3a, x3b)[h])):
            for b in range(blocks):
                xall[b, halves(h), j * BLK : (j + 1) * BLK] = source[:, b * BLK : (b + 1) * BLK]

    def picked(here, f):
        return jnp.concatenate([xall[links[row_blocks + blocks + f], here, :], lat[here, :]], axis=1)

    curve = math.sqrt(2.0 / math.pi)

    def forward(h, first, count):
        here = slice(h * mid_rows, (h + 1) * mid_rows)

        def one(f):
            fr = block_of(f)
            wl = jnp.concatenate([wv[fr, :], leftv[fr, :]], axis=1)
            pre = lax.dot_general(picked(halves(h), f), wl, (((1,), (1,)), ((), ())), preferred_element_type=F32)
            square = pre * pre
            th = jnp.tanh(curve * (pre + 0.044715 * (square * pre)))
            cdf = 0.5 + 0.5 * th
            actv[here, fr] = (pre * cdf).astype(BF16)
            slope = cdf + (0.5 * curve) * pre * (1.0 - th * th) * (1.0 + (3.0 * 0.044715) * square)
            gp[here, fr] = (gp[here, fr].astype(F32) * slope).astype(BF16)

        loop(first, count, one)

    def spread(h):
        here = slice(h * mid_rows, (h + 1) * mid_rows)

        def one(f):
            fr = block_of(f)
            sums[f] = sums[links[f]] + jnp.dot(gp[here, fr], wv[fr, :], preferred_element_type=F32)

        loop(0, row_blocks, one)
        for b in range(blocks):
            total = sums[links[row_blocks + b]].astype(BF16)
            for j in range(LEVELS):
                terms[j, here, b * BLK : (b + 1) * BLK] = total[:, j * BLK : (j + 1) * BLK]

    first = [remote(at(terms.at[1], c), at(rx1, c), x1s.at[c], x1r.at[c], back, s) for c in range(FEATS)]
    second = [remote(at(rx1, c), at(rx2, c), x2s.at[c], x2r.at[c], side, s) for c in range(FEATS)]
    upward = [remote(at(terms.at[3], c), at(rz, c), zs.at[c], zr.at[c], up, s) for c in range(FEATS)]

    def send_terms(c):
        first[c].start()
        upward[c].start()

    def hand_on(c):
        here = slice(c * slab, (c + 1) * slab)
        first[c].wait_recv()
        rx1[here, :] = (terms[2, here, :].astype(F32) + rx1[here, :].astype(F32)).astype(BF16)
        second[c].start()

    latent.finish()
    for c in range(FEATS):
        lat[c * slab : (c + 1) * slab, :] = shared[c]
    for c in range(4):
        passed[c].wait_recv()
        across[c].wait_recv()
    for copy in loads[1:]:
        copy.wait()
    repack(0)
    forward(0, 0, 8)
    relay(5)
    forward(0, 8, 8)
    relay(6)
    forward(0, 16, 8)
    relay(7)
    forward(0, 24, row_blocks - 24)
    spread(0)
    for c in range(4):
        own[4 + c].wait_send()
        send_terms(c)
    for c in range(4, FEATS):
        passed[c].wait_recv()
        across[c].wait_recv()
    repack(1)
    forward(1, 0, 16)
    hand_on(0)
    forward(1, 16, row_blocks - 16)
    hand_on(1)
    act_out = pltpu.make_async_copy(actv, act_hbm, act_sem)
    act_out.start()
    for c in range(FEATS):
        part[c] = jnp.dot(gp[c * slab : (c + 1) * slab, :], leftv[...], preferred_element_type=F32)
    latent.drain()
    back_sum = FeatSum(p, s, part, outgoing, landed2, shared2, (rs_send2, rs_recv2, ag_send2, ag_recv2))
    back_sum.send()

    def seq_at(half_, y_, core_):
        return half_ * 8 + y_ * 2 + core_

    def grad_rows(first_block, count):
        def one(f):
            fr = block_of(f)
            xl = picked(slice(0, rows), f)
            grads[fr, :] = (
                lax.dot_general(gp[:, fr], xl, (((0,), (0,)), ((), ())), preferred_element_type=F32) * norm_scale
            ).astype(BF16)

        loop(first_block, count, one)

    slots = [(dy, h) for dy in (2, 1, 3, 0) for h in (0, 1)]

    def rows_of(dy, h, core_):
        there = half if h == 1 else 1 - half
        return pl.ds(pl.multiple_of(seq_at(there, (y + dy) % 4, core_) * piece, 32), piece)

    sibling = seq_at(half, y, 1 - core)
    up_y, down_y = seq_at(half, (y + 1) % 4, core), seq_at(half, (y + 3) % 4, core)
    other_half = seq_at(1 - half, y, core)
    cores = [
        remote(grads.at[rows_of(dy, h, 1 - core), :], crecv.at[i], cs.at[i], cr.at[i], p, sibling)
        for i, (dy, h) in enumerate(slots)
    ]
    far = [
        remote(q.at[0], ry2.at[0], y2s.at[0], y2r.at[0], p, up_y),
        remote(q.at[1], ry2.at[1], y2s.at[1], y2r.at[1], p, down_y),
    ]
    near = [remote(q.at[2 + i], ry1.at[i], y1s.at[i], y1r.at[i], p, up_y if i < 2 else down_y) for i in range(4)]

    def pair_sum(i):
        dy, h = slots[i]
        cores[i].wait_recv()
        q[i] = (grads[rows_of(dy, h, core), :].astype(F32) + crecv[i].astype(F32)).astype(BF16)

    far_pair = ((y + 2) % 4) // 2
    per_pair = row_blocks // 4
    for h in (0, 1):
        grad_rows(far_pair * per_pair + h * 2 * per_pair, per_pair)
    cores[0].start()
    cores[1].start()
    hand_on(2)
    hand_on(3)
    spread(1)
    for c in (4, 5, 6):
        send_terms(c)
    for i in range(2):
        pair_sum(i)
        far[i].start()
    back_sum.share()
    for h in (0, 1):
        grad_rows((1 - far_pair) * per_pair + h * 2 * per_pair, per_pair)
    for copy in cores[2:]:
        copy.start()
    send_terms(7)
    pair_sum(3)
    near[1].start()
    pair_sum(4)
    near[2].start()
    hand_on(4)
    pair_sum(2)
    pair_sum(5)
    back_sum.finish()
    for c in range(FEATS):
        backv[c * slab : (c + 1) * slab, :] = shared2[c]
    product = lax.dot_general(tokv[...], backv[...], (((0,), (0,)), ((), ())), preferred_element_type=F32) * norm_scale
    grow = gright.shape[0]
    for k in range(SEQS):
        grsend[k] = product[k * grow : (k + 1) * grow, :].astype(BF16)
    rights = [
        remote(grsend.at[(s + k) % SEQS], grrecv.at[k - 1], gs.at[k - 1], gr.at[k - 1], p, (s + k) % SEQS)
        for k in range(1, SEQS)
    ]
    for copy in rights:
        copy.start()
    hand_on(5)
    far[0].wait_recv()
    q[2] = (q[2].astype(F32) + ry2[0].astype(F32)).astype(BF16)
    near[0].start()
    far[1].wait_recv()
    q[5] = (q[5].astype(F32) + ry2[1].astype(F32)).astype(BF16)
    near[3].start()
    hand_on(6)
    hand_on(7)
    pair_sum(6)
    pair_sum(7)
    for c in range(FEATS):
        here = slice(c * slab, (c + 1) * slab)
        low = lax.dot_general(backv[here, :], right[...], (((1,), (1,)), ((), ())), preferred_element_type=F32)
        second[c].wait_recv()
        upward[c].wait_recv()
        terms[0, here, :] = (
            low + terms[0, here, :].astype(F32) + rx2[here, :].astype(F32) + rz[here, :].astype(F32)
        ).astype(BF16)
    regroup = []
    for k in range(1, FEATS):
        there = (p + k) % FEATS
        mine_rows = pl.ds(pl.multiple_of(there * slab, slab), slab)
        regroup.append(
            remote(terms.at[0, mine_rows, :], a2a.at[p], as_.at[k - 1], ar.at[k - 1], there, s)
        )
    for copy in regroup:
        copy.start()
    a2a[p] = terms[0, pl.ds(pl.multiple_of(p * slab, slab), slab), :]
    for copy in near:
        copy.wait_recv()
    zsend[...] = (q[6].astype(F32) + ry1[0].astype(F32) + ry1[2].astype(F32)).astype(BF16)
    cross = remote(zsend, zrecv, hs, hr, p, other_half)
    cross.start()
    total = grsend[s].astype(F32)
    for k, copy in enumerate(rights):
        copy.wait_recv()
        total = total + grrecv[k].astype(F32)
    gright[...] = total
    cross.wait_recv()
    grad[...] = q[7].astype(F32) + ry1[1].astype(F32) + ry1[3].astype(F32) + zrecv[...].astype(F32)
    for copy in regroup:
        copy.wait_recv()
    back_sum.drain()
    for copy in own[:4] + passed + across + first + second + upward + cores + far + near + rights + regroup + [cross]:
        copy.wait_send()
    act_out.wait()


def chain_links(pattern, blocks):
    count = pattern.shape[0]
    places = pattern[:, 0] % blocks
    rows = jnp.arange(count)
    wanted = jnp.concatenate([places, jnp.arange(blocks, dtype=places.dtype)])
    limit = jnp.concatenate([rows, jnp.full((blocks,), count)])
    found = (wanted[:, None] == places[None, :]) & (rows[None, :] < limit[:, None])
    latest = jnp.max(jnp.where(found, rows[None, :], -1), axis=1)
    return jnp.concatenate([jnp.where(latest < 0, count, latest), places]).astype(jnp.int32)


def fused(tokens, weights, left, right, pattern, cotangent, norm_scale):
    rows, width = tokens.shape
    out_rows, wide = weights.shape
    rank = left.shape[1]
    slab = rows // FEATS
    row_blocks, blocks = out_rows // BLK, width // BLK
    piece, grow = out_rows // SEQS, width // SEQS
    all_wide = wide + rank
    any_spec = pl.BlockSpec(memory_space=pl.ANY)
    vmem_spec = pl.BlockSpec(memory_space=pltpu.VMEM)
    smem_spec = pl.BlockSpec(memory_space=pltpu.SMEM)
    dma = pltpu.SemaphoreType.DMA
    d8, d7, d4, d2, d15 = dma((8,)), dma((7,)), dma((4,)), dma((2,)), dma((15,))
    half = pltpu.VMEM((rows // 2, width), BF16)
    whole = pltpu.VMEM((rows, width), BF16)
    slabs, slabs7 = pltpu.VMEM((FEATS, slab, rank), BF16), pltpu.VMEM((FEATS - 1, slab, rank), BF16)
    flat = pltpu.VMEM((rows, rank), BF16)
    return pl.pallas_call(
        functools.partial(kernel, norm_scale),
        out_shape=(
            jax.ShapeDtypeStruct((rows, out_rows), BF16),
            jax.ShapeDtypeStruct((FEATS, slab, width), BF16),
            jax.ShapeDtypeStruct((piece, all_wide), F32),
            jax.ShapeDtypeStruct((grow, rank), F32),
        ),
        in_specs=[smem_spec, any_spec, any_spec, any_spec, any_spec, vmem_spec],
        out_specs=(any_spec, vmem_spec, vmem_spec, vmem_spec),
        scratch_shapes=[
            pltpu.VMEM((blocks, rows, wide), BF16),
            whole, half, half, half, half, half, half,
            pltpu.VMEM((out_rows, wide), BF16), pltpu.VMEM((out_rows, rank), BF16),
            pltpu.VMEM((rows, out_rows), BF16), pltpu.VMEM((rows, out_rows), BF16),
            pltpu.VMEM((row_blocks + 1, rows // 2, wide), F32),
            pltpu.VMEM((LEVELS, rows, width), BF16),
            pltpu.VMEM((out_rows, all_wide), BF16),
            pltpu.VMEM((FEATS, slab, rank), F32), slabs, slabs7, slabs, flat, slabs7, slabs, flat,
            whole, whole, whole,
            pltpu.VMEM((8, piece, all_wide), BF16), pltpu.VMEM((8, piece, all_wide), BF16),
            pltpu.VMEM((2, piece, all_wide), BF16), pltpu.VMEM((4, piece, all_wide), BF16),
            pltpu.VMEM((piece, all_wide), BF16), pltpu.VMEM((piece, all_wide), BF16),
            pltpu.VMEM((SEQS, grow, rank), BF16), pltpu.VMEM((SEQS - 1, grow, rank), BF16),
            d4, d8, d8, d8, d8, d8, d8, d7, d7, d7, d7, d7, d7, d7, d7,
            d8, d8, d8, d8, d8, d8, d7, d7, d8, d8, d2, d2, d4, d4, dma, dma, d15, d15, dma,
        ],
        compiler_params=pltpu.CompilerParams(collective_id=0, has_side_effects=True, vmem_limit_bytes=VMEM_LIMIT),
    )(chain_links(pattern, blocks), tokens, weights, left, cotangent, right)


def place_kernel(wide, act, a2a, grad, gright, act_o, gin_o, gb_o, gl_o, gr_o, actv, a2av, gradv, grv, in_sem, out_sem):
    parts = 4
    step = act.shape[0] // parts
    width = a2a.shape[2]
    rows = [pl.ds(i * step, step) for i in range(parts)]
    moves = [(act.at[r, :], actv.at[r, :], [(actv.at[r, :], act_o.at[r, :])]) for r in rows]
    moves.append(
        (grad, gradv, [(gradv.at[:, pl.ds(0, wide)], gb_o), (gradv.at[:, pl.ds(wide, gradv.shape[1] - wide)], gl_o)])
    )
    moves.append((gright, grv, [(grv, gr_o)]))
    moves += [
        (a2a.at[c], a2av.at[c], [(a2av.at[c], gin_o.at[:, pl.ds(c * width, width)])]) for c in range(a2a.shape[0])
    ]
    ins = [pltpu.make_async_copy(src, mid, in_sem.at[i]) for i, (src, mid, _) in enumerate(moves)]
    for copy in ins:
        copy.start()
    outs = []
    for copy, (_, _, after) in zip(ins, moves):
        copy.wait()
        for src, dst in after:
            outs.append(pltpu.make_async_copy(src, dst, out_sem.at[len(outs)]))
            outs[-1].start()
    for copy in outs:
        copy.wait()


def place(act, a2a, grad, gright, wide):
    any_spec = pl.BlockSpec(memory_space=pl.ANY)
    feats, slab, width = a2a.shape
    piece, all_wide = grad.shape
    dma = pltpu.SemaphoreType.DMA
    return pl.pallas_call(
        functools.partial(place_kernel, wide),
        out_shape=(
            jax.ShapeDtypeStruct(act.shape, BF16),
            jax.ShapeDtypeStruct((slab, feats * width), BF16),
            jax.ShapeDtypeStruct((piece, wide), F32),
            jax.ShapeDtypeStruct((piece, all_wide - wide), F32),
            jax.ShapeDtypeStruct(gright.shape, F32),
        ),
        in_specs=[any_spec] * 4,
        out_specs=(any_spec,) * 5,
        scratch_shapes=[
            pltpu.VMEM(act.shape, BF16), pltpu.VMEM(a2a.shape, BF16),
            pltpu.VMEM(grad.shape, F32), pltpu.VMEM(gright.shape, F32),
            dma((14,)), dma((15,)),
        ],
        compiler_params=pltpu.CompilerParams(vmem_limit_bytes=16 * 1024 * 1024),
    )(act, a2a, grad, gright)


def local(tokens, block_weights, left_factor, right_factor, pattern, cotangent):
    norm_scale = 1.0 / math.sqrt(tokens.shape[0] * lax.axis_size("seq"))
    act, a2a, grad, gright = fused(
        tokens, block_weights, left_factor, right_factor, pattern, cotangent, norm_scale
    )
    activated, grad_input, grad_blocks, grad_left, grad_right = place(act, a2a, grad, gright, block_weights.shape[1])
    return activated, grad_input[None], grad_blocks, grad_left, grad_right


def solution(mesh):
    in_specs = (
        P("seq", "feat"),
        P("feat", None),
        P("feat", None),
        P("feat", None),
        P("feat", None),
        P("seq", "feat"),
    )
    out_specs = (
        P("seq", "feat"),
        P("seq", "feat", None),
        P(("feat", "seq"), None),
        P(("feat", "seq"), None),
        P(("feat", "seq"), None),
    )
    return jax.shard_map(local, mesh=mesh, in_specs=in_specs, out_specs=out_specs, check_vma=False)
```

```python
import functools
import math

import jax
import jax.numpy as jnp
from jax import lax
from jax.experimental import pallas as pl
from jax.experimental.pallas import tpu as pltpu
from jax.sharding import PartitionSpec as P

BLK = 128
LEVELS = 4
FEATS = 8
SEQS = 16
UNROLL = 4
MESH = pl.DeviceIdType.MESH
F32 = jnp.float32
BF16 = jnp.bfloat16
VMEM_LIMIT = 67043328


def remote(src, dst, send_sem, recv_sem, feat, seq):
    return pltpu.make_async_remote_copy(
        src_ref=src,
        dst_ref=dst,
        send_sem=send_sem,
        recv_sem=recv_sem,
        device_id=(feat, seq),
        device_id_type=MESH,
    )


def greet(devices):
    barrier = pltpu.get_barrier_semaphore()
    for feat, seq in devices:
        pl.semaphore_signal(barrier, inc=1, device_id=(feat, seq), device_id_type=MESH)
    pl.semaphore_wait(barrier, len(devices))


class FeatSum:
    def __init__(self, p, s, part, outgoing, landed, shared, sems):
        rs_send, rs_recv, ag_send, ag_recv = sems
        self.p, self.part, self.outgoing, self.landed, self.shared = p, part, outgoing, landed, shared
        self.rs, self.ag = [], []
        for k in range(1, FEATS):
            there = (p + k) % FEATS
            self.rs.append(
                remote(outgoing.at[there], landed.at[k - 1], rs_send.at[k - 1], rs_recv.at[k - 1], there, s)
            )
            self.ag.append(remote(shared.at[p], shared.at[p], ag_send.at[k - 1], ag_recv.at[k - 1], there, s))

    def send(self):
        self.outgoing[...] = self.part[...].astype(BF16)
        for copy in self.rs:
            copy.start()

    def share(self):
        total = self.part[self.p]
        for k, copy in enumerate(self.rs):
            copy.wait_recv()
            total = total + self.landed[k].astype(F32)
        self.shared[self.p] = total.astype(BF16)
        for copy in self.ag:
            copy.start()

    def finish(self):
        for copy in self.ag:
            copy.wait_recv()

    def drain(self):
        for copy in self.rs + self.ag:
            copy.wait_send()


def loop(first, count, fn):
    def body(i, carry):
        for u in range(UNROLL):
            fn(first + i * UNROLL + u)
        return carry

    lax.fori_loop(0, count // UNROLL, body, 0)
    for u in range(count % UNROLL):
        fn(first + count - count % UNROLL + u)


def block_of(f):
    start = f * BLK
    return pl.ds(start if isinstance(start, int) else pl.multiple_of(start, BLK), BLK)


def kernel(norm_scale, *refs):
    (links, tok, w_hbm, left_hbm, cot_hbm, right) = refs[:6]
    (act_hbm, a2a, grad, gright) = refs[6:10]
    (
        xall, tokv, x1a, x1b, x2a, x2b, x3a, x3b, wv, leftv, gp, actv, sums, terms, grads,
        part, outgoing, landed, shared, lat, backp, backo, backl, backs, backv, rx1, rx2, rz,
        crecv, q, ry2, ry1, zsend, zrecv, grsend, grrecv,
    ) = refs[10:46]
    (
        lsem, x_send, x_recv, f_send, f_recv, z_send, z_recv, rs_send, rs_recv, ag_send, ag_recv,
        rs_send2, rs_recv2, ag_send2, ag_recv2, x1s, x1r, x2s, x2r, zs, zr, as_, ar,
        cs, cr, y2s, y2r, y1s, y1r, hs, hr, gs, gr, act_sem,
    ) = refs[46:]
    p, s = lax.axis_index("feat"), lax.axis_index("seq")
    x, z = p // 2, p % 2
    side, back, up = 2 * (x + 1 - 2 * (x % 2)) + z, 2 * (3 - x) + z, 2 * x + 1 - z
    core, y, half = s % 2, (s // 2) % 4, s // 8
    slab, rank = part.shape[1], part.shape[2]
    small, width = tokv.shape[2], tokv.shape[3]
    rows = FEATS * slab
    mid_rows = rows // 2
    blocks = width // BLK
    row_blocks = wv.shape[0] // BLK
    wide = LEVELS * BLK
    piece = q.shape[1]

    def part_of(ref, h, c):
        return ref.at[pl.ds(h * mid_rows + c * small, small), :]

    tok_loads = [pltpu.make_async_copy(tok.at[:, h], tokv.at[h], lsem.at[h]) for h in range(2)]
    loads = [pltpu.make_async_copy(w_hbm, wv, lsem.at[2]), pltpu.make_async_copy(left_hbm, leftv, lsem.at[3])]
    for h in range(2):
        for c in range(FEATS):
            loads.append(
                pltpu.make_async_copy(cot_hbm.at[c, h], part_of(gp, h, c), lsem.at[4 + h * FEATS + c])
            )
    for copy in tok_loads + loads:
        copy.start()
    greet([((p + k) % FEATS, s) for k in range(1, FEATS)] + [(p, (s + k) % SEQS) for k in range(1, SEQS)])

    def chunk(pair, c):
        return pair[c // 4].at[pl.ds((c % 4) * 2, 2)]

    def own_chunk(c):
        return tok.at[pl.ds((c % 4) * 2, 2), c // 4]

    def at(ref, c):
        return ref.at[pl.ds(c * slab, slab), :]

    own = [remote(own_chunk(c), chunk((x2a, x2b), c), x_send.at[c], x_recv.at[c], side, s) for c in range(FEATS)]
    passed = [
        remote(chunk((x2a, x2b), c), chunk((x1a, x1b), c), f_send.at[c], f_recv.at[c], back, s) for c in range(FEATS)
    ]
    across = [remote(own_chunk(c), chunk((x3a, x3b), c), z_send.at[c], z_recv.at[c], up, s) for c in range(FEATS)]
    latent = FeatSum(p, s, part, outgoing, landed, shared, (rs_send, rs_recv, ag_send, ag_recv))
    own[0].start()
    across[0].start()
    for copy in tok_loads:
        copy.wait()
    for c in range(FEATS):
        mine = tokv[c // 4, (c % 4) * 2 : (c % 4) * 2 + 2].reshape(slab, width)
        part[c] = jnp.dot(mine, right[...], preferred_element_type=F32)
    latent.send()
    for c in (1,):
        own[c].start()
        across[c].start()

    sums[row_blocks] = jnp.zeros(sums.shape[1:], F32)

    def relay(c):
        own[c].wait_recv()
        passed[c].start()
        if c + 2 < FEATS:
            own[c + 2].start()
            across[c + 2].start()

    relay(0)
    latent.share()
    for c in range(1, 5):
        relay(c)

    def halves(h):
        return slice(h * mid_rows, (h + 1) * mid_rows)

    def repack(h):
        for j, source in enumerate((tokv.at[h], (x1a, x1b)[h], (x2a, x2b)[h], (x3a, x3b)[h])):
            for b in range(blocks):
                block = source[:, :, b * BLK : (b + 1) * BLK].reshape(mid_rows, BLK)
                xall[b, halves(h), j * BLK : (j + 1) * BLK] = block

    def picked(here, f):
        return jnp.concatenate([xall[links[row_blocks + blocks + f], here, :], lat[here, :]], axis=1)

    curve = math.sqrt(2.0 / math.pi)

    def forward(h, first, count):
        here = slice(h * mid_rows, (h + 1) * mid_rows)

        def one(f):
            fr = block_of(f)
            wl = jnp.concatenate([wv[fr, :], leftv[fr, :]], axis=1)
            pre = lax.dot_general(picked(halves(h), f), wl, (((1,), (1,)), ((), ())), preferred_element_type=F32)
            square = pre * pre
            th = jnp.tanh(curve * (pre + 0.044715 * (square * pre)))
            cdf = 0.5 + 0.5 * th
            actv[here, fr] = (pre * cdf).astype(BF16)
            slope = cdf + (0.5 * curve) * pre * (1.0 - th * th) * (1.0 + (3.0 * 0.044715) * square)
            gp[here, fr] = (gp[here, fr].astype(F32) * slope).astype(BF16)

        loop(first, count, one)

    def spread(h, begin, count):
        here = slice(h * mid_rows, (h + 1) * mid_rows)

        def one(f):
            fr = block_of(f)
            sums[f] = sums[links[f]] + jnp.dot(gp[here, fr], wv[fr, :], preferred_element_type=F32)

        loop(begin, count, one)

    def collect(h):
        here = slice(h * mid_rows, (h + 1) * mid_rows)
        for b in range(blocks):
            total = sums[links[row_blocks + b]].astype(BF16)
            for j in range(LEVELS):
                terms[j, here, b * BLK : (b + 1) * BLK] = total[:, j * BLK : (j + 1) * BLK]

    first = [remote(at(terms.at[1], c), at(rx1, c), x1s.at[c], x1r.at[c], back, s) for c in range(FEATS)]
    second = [remote(at(rx1, c), at(rx2, c), x2s.at[c], x2r.at[c], side, s) for c in range(FEATS)]
    upward = [remote(at(terms.at[3], c), at(rz, c), zs.at[c], zr.at[c], up, s) for c in range(FEATS)]

    def send_terms(c):
        first[c].start()
        upward[c].start()

    def hand_on(c):
        here = slice(c * slab, (c + 1) * slab)
        first[c].wait_recv()
        rx1[here, :] = (terms[2, here, :].astype(F32) + rx1[here, :].astype(F32)).astype(BF16)
        second[c].start()

    def back_sum_of(h):
        return FeatSum(
            p, s, backp.at[h], backo.at[h], backl.at[h], backs.at[h],
            (rs_send2.at[h], rs_recv2.at[h], ag_send2.at[h], ag_recv2.at[h]),
        )

    back_sums = [back_sum_of(0), back_sum_of(1)]

    def start_back(h):
        for c in range(FEATS):
            here = slice(h * mid_rows + c * small, h * mid_rows + (c + 1) * small)
            if c % 4 == 0:
                wider = slice(h * mid_rows + c * small, h * mid_rows + (c + 4) * small)
                four = jnp.dot(gp[wider, :], leftv[...], preferred_element_type=F32)
            backp[h, c] = four[(c % 4) * small : (c % 4 + 1) * small, :]
        back_sums[h].send()

    def end_back(h):
        back_sums[h].finish()
        for c in range(FEATS):
            backv[h * mid_rows + c * small : h * mid_rows + (c + 1) * small, :] = backs[h, c]

    regroup = []
    for h in range(2):
        for k in range(1, FEATS):
            there = (p + k) % FEATS
            src = terms.at[0, pl.ds(pl.multiple_of(h * mid_rows + there * small, small), small), :]
            dst = a2a.at[p, pl.ds(h * small, small), :]
            regroup.append(remote(src, dst, as_.at[h, k - 1], ar.at[h, k - 1], there, s))

    def finish_half(h):
        for c in range(h * 4, h * 4 + 4):
            here = slice(c * slab, (c + 1) * slab)
            low = lax.dot_general(backv[here, :], right[...], (((1,), (1,)), ((), ())), preferred_element_type=F32)
            second[c].wait_recv()
            upward[c].wait_recv()
            terms[0, here, :] = (
                low + terms[0, here, :].astype(F32) + rx2[here, :].astype(F32) + rz[here, :].astype(F32)
            ).astype(BF16)
        for copy in regroup[h * (FEATS - 1) : (h + 1) * (FEATS - 1)]:
            copy.start()
        a2a[p, h * small : (h + 1) * small, :] = terms[
            0, pl.ds(pl.multiple_of(h * mid_rows + p * small, small), small), :
        ]

    latent.finish()
    for c in range(FEATS):
        lat[c * slab : (c + 1) * slab, :] = shared[c]
    for c in range(4):
        passed[c].wait_recv()
        across[c].wait_recv()
    for copy in loads:
        copy.wait()
    repack(0)
    forward(0, 0, 8)
    relay(5)
    forward(0, 8, 8)
    relay(6)
    forward(0, 16, 8)
    relay(7)
    forward(0, 24, row_blocks - 24)
    spread(0, 0, row_blocks)
    collect(0)
    for c in range(4):
        send_terms(c)
    start_back(0)
    for c in range(4, FEATS):
        passed[c].wait_recv()
        across[c].wait_recv()
    repack(1)
    forward(1, 0, 16)
    hand_on(0)
    back_sums[0].share()
    forward(1, 16, row_blocks - 16)
    hand_on(1)
    act_outs = []
    for h in range(2):
        for c in range(FEATS):
            act_outs.append(
                pltpu.make_async_copy(part_of(actv, h, c), act_hbm.at[c, h], act_sem.at[h * FEATS + c])
            )
            act_outs[-1].start()

    def seq_at(half_, y_, core_):
        return half_ * 8 + y_ * 2 + core_

    def grad_rows(first_block, count):
        def one(f):
            fr = block_of(f)
            xl = picked(slice(0, rows), f)
            grads[fr, :] = (
                lax.dot_general(gp[:, fr], xl, (((0,), (0,)), ((), ())), preferred_element_type=F32) * norm_scale
            ).astype(BF16)

        loop(first_block, count, one)

    slots = [(dy, h) for dy in (2, 1, 3, 0) for h in (0, 1)]

    def rows_of(dy, h, core_):
        there = half if h == 1 else 1 - half
        return pl.ds(pl.multiple_of(seq_at(there, (y + dy) % 4, core_) * piece, 32), piece)

    sibling = seq_at(half, y, 1 - core)
    up_y, down_y = seq_at(half, (y + 1) % 4, core), seq_at(half, (y + 3) % 4, core)
    other_half = seq_at(1 - half, y, core)
    cores = [
        remote(grads.at[rows_of(dy, h, 1 - core), :], crecv.at[i], cs.at[i], cr.at[i], p, sibling)
        for i, (dy, h) in enumerate(slots)
    ]
    far = [
        remote(q.at[0], ry2.at[0], y2s.at[0], y2r.at[0], p, up_y),
        remote(q.at[1], ry2.at[1], y2s.at[1], y2r.at[1], p, down_y),
    ]
    near = [remote(q.at[2 + i], ry1.at[i], y1s.at[i], y1r.at[i], p, up_y if i < 2 else down_y) for i in range(4)]

    def pair_sum(i):
        dy, h = slots[i]
        cores[i].wait_recv()
        q[i] = (grads[rows_of(dy, h, core), :].astype(F32) + crecv[i].astype(F32)).astype(BF16)

    far_pair = ((y + 2) % 4) // 2
    per_pair = row_blocks // 4
    for h in (0, 1):
        grad_rows(far_pair * per_pair + h * 2 * per_pair, per_pair)
    cores[0].start()
    cores[1].start()
    hand_on(2)
    spread(1, 0, row_blocks // 2)
    for i in range(2):
        pair_sum(i)
        far[i].start()
    hand_on(3)
    spread(1, row_blocks // 2, row_blocks - row_blocks // 2)
    collect(1)
    for c in (4, 5, 6, 7):
        send_terms(c)
    for h in (0, 1):
        grad_rows((1 - far_pair) * per_pair + h * 2 * per_pair, per_pair)
    for copy in cores[2:]:
        copy.start()
    start_back(1)
    end_back(0)
    pair_sum(3)
    near[1].start()
    pair_sum(4)
    near[2].start()
    pair_sum(2)
    pair_sum(5)
    hand_on(4)
    finish_half(0)
    back_sums[1].share()
    far[0].wait_recv()
    q[2] = (q[2].astype(F32) + ry2[0].astype(F32)).astype(BF16)
    near[0].start()
    far[1].wait_recv()
    q[5] = (q[5].astype(F32) + ry2[1].astype(F32)).astype(BF16)
    near[3].start()
    hand_on(5)
    hand_on(6)
    pair_sum(6)
    pair_sum(7)
    hand_on(7)
    end_back(1)
    product = (
        lax.dot_general(
            tokv[...].reshape(rows, width), backv[...], (((0,), (0,)), ((), ())), preferred_element_type=F32
        )
        * norm_scale
    )
    grow = gright.shape[0]
    for k in range(SEQS):
        grsend[k] = product[k * grow : (k + 1) * grow, :].astype(BF16)
    rights = [
        remote(grsend.at[(s + k) % SEQS], grrecv.at[k - 1], gs.at[k - 1], gr.at[k - 1], p, (s + k) % SEQS)
        for k in range(1, SEQS)
    ]
    for copy in rights:
        copy.start()
    finish_half(1)
    for copy in near:
        copy.wait_recv()
    zsend[...] = (q[6].astype(F32) + ry1[0].astype(F32) + ry1[2].astype(F32)).astype(BF16)
    cross = remote(zsend, zrecv, hs, hr, p, other_half)
    cross.start()
    total = grsend[s].astype(F32)
    for k, copy in enumerate(rights):
        copy.wait_recv()
        total = total + grrecv[k].astype(F32)
    gright[...] = total
    cross.wait_recv()
    grad[...] = q[7].astype(F32) + ry1[1].astype(F32) + ry1[3].astype(F32) + zrecv[...].astype(F32)
    for copy in regroup:
        copy.wait_recv()
    latent.drain()
    for each in back_sums:
        each.drain()
    for copy in own + passed + across + first + second + upward + cores + far + near + rights + regroup + [cross]:
        copy.wait_send()
    for copy in act_outs:
        copy.wait()


def chain_links(pattern, blocks):
    count = pattern.shape[0]
    places = pattern[:, 0] % blocks
    rows = jnp.arange(count)
    wanted = jnp.concatenate([places, jnp.arange(blocks, dtype=places.dtype)])
    limit = jnp.concatenate([rows, jnp.full((blocks,), count)])
    found = (wanted[:, None] == places[None, :]) & (rows[None, :] < limit[:, None])
    latest = jnp.max(jnp.where(found, rows[None, :], -1), axis=1)
    return jnp.concatenate([jnp.where(latest < 0, count, latest), places]).astype(jnp.int32)


def fused(tokens, weights, left, right, pattern, cotangent, norm_scale):
    rows, width = tokens.shape
    out_rows, wide = weights.shape
    rank = left.shape[1]
    slab = rows // FEATS
    row_blocks, blocks = out_rows // BLK, width // BLK
    piece, grow = out_rows // SEQS, width // SEQS
    all_wide = wide + rank
    any_spec = pl.BlockSpec(memory_space=pl.ANY)
    vmem_spec = pl.BlockSpec(memory_space=pltpu.VMEM)
    smem_spec = pl.BlockSpec(memory_space=pltpu.SMEM)
    dma = pltpu.SemaphoreType.DMA
    d8, d7, d4, d2, d15, d27 = dma((8,)), dma((7,)), dma((4,)), dma((2,)), dma((15,)), dma((2, 7))
    small = slab // 2
    half = pltpu.VMEM((FEATS, small, width), BF16)
    whole = pltpu.VMEM((rows, width), BF16)
    slabs, slabs7 = pltpu.VMEM((FEATS, slab, rank), BF16), pltpu.VMEM((FEATS - 1, slab, rank), BF16)
    flat = pltpu.VMEM((rows, rank), BF16)
    return pl.pallas_call(
        functools.partial(kernel, norm_scale),
        out_shape=(
            jax.ShapeDtypeStruct((FEATS, 2, slab // 2, out_rows), BF16),
            jax.ShapeDtypeStruct((FEATS, slab, width), BF16),
            jax.ShapeDtypeStruct((piece, all_wide), F32),
            jax.ShapeDtypeStruct((grow, rank), F32),
        ),
        in_specs=[smem_spec, any_spec, any_spec, any_spec, any_spec, vmem_spec],
        out_specs=(any_spec, vmem_spec, vmem_spec, vmem_spec),
        scratch_shapes=[
            pltpu.VMEM((blocks, rows, wide), BF16),
            pltpu.VMEM((2, FEATS, small, width), BF16), half, half, half, half, half, half,
            pltpu.VMEM((out_rows, wide), BF16), pltpu.VMEM((out_rows, rank), BF16),
            pltpu.VMEM((rows, out_rows), BF16), pltpu.VMEM((rows, out_rows), BF16),
            pltpu.VMEM((row_blocks + 1, rows // 2, wide), F32),
            pltpu.VMEM((LEVELS, rows, width), BF16),
            pltpu.VMEM((out_rows, all_wide), BF16),
            pltpu.VMEM((FEATS, slab, rank), F32), slabs, slabs7, slabs, flat,
            pltpu.VMEM((2, FEATS, small, rank), F32), pltpu.VMEM((2, FEATS, small, rank), BF16),
            pltpu.VMEM((2, FEATS - 1, small, rank), BF16), pltpu.VMEM((2, FEATS, small, rank), BF16), flat,
            whole, whole, whole,
            pltpu.VMEM((8, piece, all_wide), BF16), pltpu.VMEM((8, piece, all_wide), BF16),
            pltpu.VMEM((2, piece, all_wide), BF16), pltpu.VMEM((4, piece, all_wide), BF16),
            pltpu.VMEM((piece, all_wide), BF16), pltpu.VMEM((piece, all_wide), BF16),
            pltpu.VMEM((SEQS, grow, rank), BF16), pltpu.VMEM((SEQS - 1, grow, rank), BF16),
            dma((20,)), d8, d8, d8, d8, d8, d8, d7, d7, d7, d7, d27, d27, d27, d27,
            d8, d8, d8, d8, d8, d8, d27, d27, d8, d8, d2, d2, d4, d4, dma, dma, d15, d15, dma((16,)),
        ],
        compiler_params=pltpu.CompilerParams(collective_id=0, has_side_effects=True, vmem_limit_bytes=VMEM_LIMIT),
    )(
        chain_links(pattern, blocks),
        tokens.reshape(FEATS, 2, slab // 2, width),
        weights,
        left,
        cotangent.reshape(FEATS, 2, slab // 2, out_rows),
        right,
    )


def place_kernel(wide, act, a2a, grad, gright, act_o, gin_o, gb_o, gl_o, gr_o, actv, a2av, gradv, grv, in_sem, out_sem):
    parts = 4
    step = act.shape[0] // parts
    width = a2a.shape[2]
    rows = [pl.ds(i * step, step) for i in range(parts)]
    moves = [(act.at[r, :], actv.at[r, :], [(actv.at[r, :], act_o.at[r, :])]) for r in rows]
    moves.append(
        (grad, gradv, [(gradv.at[:, pl.ds(0, wide)], gb_o), (gradv.at[:, pl.ds(wide, gradv.shape[1] - wide)], gl_o)])
    )
    moves.append((gright, grv, [(grv, gr_o)]))
    moves += [
        (a2a.at[c], a2av.at[c], [(a2av.at[c], gin_o.at[:, pl.ds(c * width, width)])]) for c in range(a2a.shape[0])
    ]
    ins = [pltpu.make_async_copy(src, mid, in_sem.at[i]) for i, (src, mid, _) in enumerate(moves)]
    for copy in ins:
        copy.start()
    outs = []
    for copy, (_, _, after) in zip(ins, moves):
        copy.wait()
        for src, dst in after:
            outs.append(pltpu.make_async_copy(src, dst, out_sem.at[len(outs)]))
            outs[-1].start()
    for copy in outs:
        copy.wait()


def place(act, a2a, grad, gright, wide):
    any_spec = pl.BlockSpec(memory_space=pl.ANY)
    feats, slab, width = a2a.shape
    piece, all_wide = grad.shape
    dma = pltpu.SemaphoreType.DMA
    return pl.pallas_call(
        functools.partial(place_kernel, wide),
        out_shape=(
            jax.ShapeDtypeStruct(act.shape, BF16),
            jax.ShapeDtypeStruct((slab, feats * width), BF16),
            jax.ShapeDtypeStruct((piece, wide), F32),
            jax.ShapeDtypeStruct((piece, all_wide - wide), F32),
            jax.ShapeDtypeStruct(gright.shape, F32),
        ),
        in_specs=[any_spec] * 4,
        out_specs=(any_spec,) * 5,
        scratch_shapes=[
            pltpu.VMEM(act.shape, BF16), pltpu.VMEM(a2a.shape, BF16),
            pltpu.VMEM(grad.shape, F32), pltpu.VMEM(gright.shape, F32),
            dma((14,)), dma((15,)),
        ],
        compiler_params=pltpu.CompilerParams(vmem_limit_bytes=VMEM_LIMIT),
    )(act, a2a, grad, gright)


def local(tokens, block_weights, left_factor, right_factor, pattern, cotangent):
    norm_scale = 1.0 / math.sqrt(tokens.shape[0] * lax.axis_size("seq"))
    act, a2a, grad, gright = fused(
        tokens, block_weights, left_factor, right_factor, pattern, cotangent, norm_scale
    )
    activated, grad_input, grad_blocks, grad_left, grad_right = place(
        act.reshape(cotangent.shape), a2a, grad, gright, block_weights.shape[1]
    )
    return activated, grad_input[None], grad_blocks, grad_left, grad_right


def solution(mesh):
    in_specs = (
        P("seq", "feat"),
        P("feat", None),
        P("feat", None),
        P("feat", None),
        P("feat", None),
        P("seq", "feat"),
    )
    out_specs = (
        P("seq", "feat"),
        P("seq", "feat", None),
        P(("feat", "seq"), None),
        P(("feat", "seq"), None),
        P(("feat", "seq"), None),
    )
    return jax.shard_map(local, mesh=mesh, in_specs=in_specs, out_specs=out_specs, check_vma=False)
```

```python
import functools
import math

import jax
import jax.numpy as jnp
from jax import lax
from jax.experimental import pallas as pl
from jax.experimental.pallas import tpu as pltpu
from jax.sharding import PartitionSpec as P

BLK = 128
LEVELS = 4
FEATS = 8
SEQS = 16
UNROLL = 4
MESH = pl.DeviceIdType.MESH
F32 = jnp.float32
BF16 = jnp.bfloat16
VMEM_LIMIT = 67043328


def remote(src, dst, send_sem, recv_sem, feat, seq):
    return pltpu.make_async_remote_copy(
        src_ref=src,
        dst_ref=dst,
        send_sem=send_sem,
        recv_sem=recv_sem,
        device_id=(feat, seq),
        device_id_type=MESH,
    )


def greet(devices):
    barrier = pltpu.get_barrier_semaphore()
    for feat, seq in devices:
        pl.semaphore_signal(barrier, inc=1, device_id=(feat, seq), device_id_type=MESH)
    pl.semaphore_wait(barrier, len(devices))


class FeatSum:
    def __init__(self, p, s, part, outgoing, landed, shared, sems):
        rs_send, rs_recv, ag_send, ag_recv = sems
        self.p, self.part, self.outgoing, self.landed, self.shared = p, part, outgoing, landed, shared
        self.rs, self.ag = [], []
        for k in range(1, FEATS):
            there = (p + k) % FEATS
            self.rs.append(
                remote(outgoing.at[there], landed.at[k - 1], rs_send.at[k - 1], rs_recv.at[k - 1], there, s)
            )
            self.ag.append(remote(shared.at[p], shared.at[p], ag_send.at[k - 1], ag_recv.at[k - 1], there, s))

    def send(self):
        self.outgoing[...] = self.part[...].astype(BF16)
        for copy in self.rs:
            copy.start()

    def share(self):
        total = self.part[self.p]
        for k, copy in enumerate(self.rs):
            copy.wait_recv()
            total = total + self.landed[k].astype(F32)
        self.shared[self.p] = total.astype(BF16)
        for copy in self.ag:
            copy.start()

    def finish(self):
        for copy in self.ag:
            copy.wait_recv()

    def drain(self):
        for copy in self.rs + self.ag:
            copy.wait_send()


def loop(first, count, fn):
    def body(i, carry):
        for u in range(UNROLL):
            fn(first + i * UNROLL + u)
        return carry

    lax.fori_loop(0, count // UNROLL, body, 0)
    for u in range(count % UNROLL):
        fn(first + count - count % UNROLL + u)


def block_of(f):
    start = f * BLK
    return pl.ds(start if isinstance(start, int) else pl.multiple_of(start, BLK), BLK)


def kernel(norm_scale, *refs):
    (links, tok, w_hbm, left_hbm, cot_hbm, right) = refs[:6]
    (act_hbm, a2a, grad, gright) = refs[6:10]
    (
        xall, tokv, x1a, x1b, x2a, x2b, x3a, x3b, wv, leftv, gp, actv, sums, terms, grads,
        part, outgoing, landed, shared, lat, backp, backo, backl, backs, backv, rx1, rx2, rz,
        crecv, q, ry2, ry1, zsend, zrecv, grsend, grpair, grsum, grrecv,
    ) = refs[10:48]
    (
        lsem, x_send, x_recv, f_send, f_recv, z_send, z_recv, rs_send, rs_recv, ag_send, ag_recv,
        rs_send2, rs_recv2, ag_send2, ag_recv2, x1s, x1r, x2s, x2r, zs, zr, as_, ar,
        cs, cr, y2s, y2r, y1s, y1r, hs, hr, gps, gpr, gs, gr, act_sem,
    ) = refs[48:]
    p, s = lax.axis_index("feat"), lax.axis_index("seq")
    x, z = p // 2, p % 2
    side, back, up = 2 * (x + 1 - 2 * (x % 2)) + z, 2 * (3 - x) + z, 2 * x + 1 - z
    core, y, half = s % 2, (s // 2) % 4, s // 8
    slab, rank = part.shape[1], part.shape[2]
    small, width = tokv.shape[2], tokv.shape[3]
    rows = FEATS * slab
    mid_rows = rows // 2
    blocks = width // BLK
    row_blocks = wv.shape[0] // BLK
    wide = LEVELS * BLK
    piece = crecv.shape[1]

    def part_of(ref, h, c):
        return ref.at[pl.ds(h * mid_rows + c * small, small), :]

    tok_loads = [pltpu.make_async_copy(tok.at[:, h], tokv.at[h], lsem.at[h]) for h in range(2)]
    loads = [pltpu.make_async_copy(w_hbm, wv, lsem.at[2]), pltpu.make_async_copy(left_hbm, leftv, lsem.at[3])]
    for h in range(2):
        for c in range(FEATS):
            loads.append(
                pltpu.make_async_copy(cot_hbm.at[c, h], part_of(gp, h, c), lsem.at[4 + h * FEATS + c])
            )
    for copy in tok_loads + loads:
        copy.start()
    greet([((p + k) % FEATS, s) for k in range(1, FEATS)] + [(p, (s + k) % SEQS) for k in range(1, SEQS)])

    def chunk(pair, c):
        return pair[c // 4].at[pl.ds((c % 4) * 2, 2)]

    def own_chunk(c):
        return tok.at[pl.ds((c % 4) * 2, 2), c // 4]

    def at(ref, c):
        return ref.at[pl.ds(c * slab, slab), :]

    own = [remote(own_chunk(c), chunk((x2a, x2b), c), x_send.at[c], x_recv.at[c], side, s) for c in range(FEATS)]
    passed = [
        remote(chunk((x2a, x2b), c), chunk((x1a, x1b), c), f_send.at[c], f_recv.at[c], back, s) for c in range(FEATS)
    ]
    across = [remote(own_chunk(c), chunk((x3a, x3b), c), z_send.at[c], z_recv.at[c], up, s) for c in range(FEATS)]
    latent = FeatSum(p, s, part, outgoing, landed, shared, (rs_send, rs_recv, ag_send, ag_recv))
    own[0].start()
    across[0].start()
    for copy in tok_loads:
        copy.wait()
    for c in range(FEATS):
        mine = tokv[c // 4, (c % 4) * 2 : (c % 4) * 2 + 2].reshape(slab, width)
        part[c] = jnp.dot(mine, right[...], preferred_element_type=F32)
    latent.send()
    for c in (1,):
        own[c].start()
        across[c].start()

    sums[0] = jnp.zeros(sums.shape[1:], F32)

    def relay(c):
        own[c].wait_recv()
        passed[c].start()
        if c + 2 < FEATS:
            own[c + 2].start()
            across[c + 2].start()

    relay(0)
    latent.share()
    for c in range(1, 5):
        relay(c)

    def halves(h):
        return slice(h * mid_rows, (h + 1) * mid_rows)

    def repack(h):
        for j, source in enumerate((tokv.at[h], (x1a, x1b)[h], (x2a, x2b)[h], (x3a, x3b)[h])):
            for b in range(blocks):
                block = source[:, :, b * BLK : (b + 1) * BLK].reshape(mid_rows, BLK)
                xall[b, halves(h), j * BLK : (j + 1) * BLK] = block

    def picked(here, f):
        return jnp.concatenate([xall[links[row_blocks + blocks + f], here, :], lat[here, :]], axis=1)

    curve = math.sqrt(2.0 / math.pi)

    def forward(h, first, count):
        here = slice(h * mid_rows, (h + 1) * mid_rows)

        def one(f):
            fr = block_of(f)
            wl = jnp.concatenate([wv[fr, :], leftv[fr, :]], axis=1)
            pre = lax.dot_general(picked(halves(h), f), wl, (((1,), (1,)), ((), ())), preferred_element_type=F32)
            square = pre * pre
            th = jnp.tanh(curve * (pre + 0.044715 * (square * pre)))
            cdf = 0.5 + 0.5 * th
            actv[here, fr] = (pre * cdf).astype(BF16)
            slope = cdf + (0.5 * curve) * pre * (1.0 - th * th) * (1.0 + (3.0 * 0.044715) * square)
            gp[here, fr] = (gp[here, fr].astype(F32) * slope).astype(BF16)

        loop(first, count, one)

    def spread(h, begin, count):
        here = slice(h * mid_rows, (h + 1) * mid_rows)

        def one(f):
            fr = block_of(f)
            sums[f + 1] = sums[links[f]] + jnp.dot(gp[here, fr], wv[fr, :], preferred_element_type=F32)

        loop(begin, count, one)

    def collect(h):
        here = slice(h * mid_rows, (h + 1) * mid_rows)
        for b in range(blocks):
            total = sums[links[row_blocks + b]].astype(BF16)
            for j in range(LEVELS):
                terms[j, here, b * BLK : (b + 1) * BLK] = total[:, j * BLK : (j + 1) * BLK]

    first = [remote(at(terms.at[1], c), at(rx1, c), x1s.at[c], x1r.at[c], back, s) for c in range(FEATS)]
    second = [remote(at(rx1, c), at(rx2, c), x2s.at[c], x2r.at[c], side, s) for c in range(FEATS)]
    upward = [remote(at(terms.at[3], c), at(rz, c), zs.at[c], zr.at[c], up, s) for c in range(FEATS)]

    def send_terms(c):
        first[c].start()
        upward[c].start()

    def hand_on(c):
        here = slice(c * slab, (c + 1) * slab)
        first[c].wait_recv()
        rx1[here, :] = (terms[2, here, :].astype(F32) + rx1[here, :].astype(F32)).astype(BF16)
        second[c].start()

    def back_sum_of(h):
        return FeatSum(
            p, s, backp.at[h], backo.at[h], backl.at[h], backs.at[h],
            (rs_send2.at[h], rs_recv2.at[h], ag_send2.at[h], ag_recv2.at[h]),
        )

    back_sums = [back_sum_of(0), back_sum_of(1)]

    def start_back(h):
        for c in range(FEATS):
            here = slice(h * mid_rows + c * small, h * mid_rows + (c + 1) * small)
            if c % 4 == 0:
                wider = slice(h * mid_rows + c * small, h * mid_rows + (c + 4) * small)
                four = jnp.dot(gp[wider, :], leftv[...], preferred_element_type=F32)
            backp[h, c] = four[(c % 4) * small : (c % 4 + 1) * small, :]
        back_sums[h].send()

    def end_back(h):
        back_sums[h].finish()
        for c in range(FEATS):
            backv[h * mid_rows + c * small : h * mid_rows + (c + 1) * small, :] = backs[h, c]

    regroup = []
    for h in range(2):
        for k in range(1, FEATS):
            there = (p + k) % FEATS
            src = terms.at[0, pl.ds(pl.multiple_of(h * mid_rows + there * small, small), small), :]
            dst = a2a.at[p, pl.ds(h * small, small), :]
            regroup.append(remote(src, dst, as_.at[h, k - 1], ar.at[h, k - 1], there, s))

    def finish_half(h):
        lows = lax.dot_general(
            backv[halves(h), :], right[...], (((1,), (1,)), ((), ())), preferred_element_type=F32
        )
        for c in range(h * 4, h * 4 + 4):
            here = slice(c * slab, (c + 1) * slab)
            low = lows[(c % 4) * slab : (c % 4 + 1) * slab, :]
            second[c].wait_recv()
            upward[c].wait_recv()
            terms[0, here, :] = (
                low + terms[0, here, :].astype(F32) + rx2[here, :].astype(F32) + rz[here, :].astype(F32)
            ).astype(BF16)
        for copy in regroup[h * (FEATS - 1) : (h + 1) * (FEATS - 1)]:
            copy.start()
        a2a[p, h * small : (h + 1) * small, :] = terms[
            0, pl.ds(pl.multiple_of(h * mid_rows + p * small, small), small), :
        ]

    latent.finish()
    for c in range(FEATS):
        lat[c * slab : (c + 1) * slab, :] = shared[c]
    for c in range(4):
        passed[c].wait_recv()
        across[c].wait_recv()
    for copy in loads:
        copy.wait()
    repack(0)
    forward(0, 0, 12)
    relay(5)
    forward(0, 12, row_blocks - 12)
    relay(6)
    spread(0, 0, row_blocks // 2)
    relay(7)
    spread(0, row_blocks // 2, row_blocks - row_blocks // 2)
    collect(0)
    start_back(0)
    send_terms(0)
    send_terms(1)
    for c in range(4, FEATS):
        passed[c].wait_recv()
        across[c].wait_recv()
    repack(1)
    forward(1, 0, 12)
    hand_on(0)
    send_terms(2)
    back_sums[0].share()
    forward(1, 12, row_blocks - 12)
    hand_on(1)
    send_terms(3)
    act_outs = []
    for h in range(2):
        for c in range(FEATS):
            act_outs.append(
                pltpu.make_async_copy(part_of(actv, h, c), act_hbm.at[c, h], act_sem.at[h * FEATS + c])
            )
            act_outs[-1].start()

    def seq_at(half_, y_, core_):
        return half_ * 8 + y_ * 2 + core_

    def grad_rows(first_block, count):
        def one(f):
            fr = block_of(f)
            xl = picked(slice(0, rows), f)
            grads[fr, :] = (
                lax.dot_general(gp[:, fr], xl, (((0,), (0,)), ((), ())), preferred_element_type=F32) * norm_scale
            ).astype(BF16)

        loop(first_block, count, one)

    slots = [(dy, h) for dy in (2, 1, 3, 0) for h in (0, 1)]

    def rows_of(dy, h, core_):
        there = half if h == 1 else 1 - half
        return pl.ds(pl.multiple_of(seq_at(there, (y + dy) % 4, core_) * piece, 32), piece)

    sibling = seq_at(half, y, 1 - core)
    up_y, down_y = seq_at(half, (y + 1) % 4, core), seq_at(half, (y + 3) % 4, core)
    other_half = seq_at(1 - half, y, core)
    cores = [
        remote(grads.at[rows_of(dy, h, 1 - core), :], crecv.at[i], cs.at[i], cr.at[i], p, sibling)
        for i, (dy, h) in enumerate(slots)
    ]
    far = [
        remote(q.at[0], ry2.at[0], y2s.at[0], y2r.at[0], p, up_y),
        remote(q.at[1], ry2.at[1], y2s.at[1], y2r.at[1], p, down_y),
    ]
    near = [remote(q.at[2 + i], ry1.at[i], y1s.at[i], y1r.at[i], p, up_y if i < 2 else down_y) for i in range(4)]

    def pair_sum(i, *others):
        dy, h = slots[i]
        total = grads[rows_of(dy, h, core), :].astype(F32) + crecv[i].astype(F32)
        for other in others:
            total = total + other[...].astype(F32)
        return total

    def send_sum(i, copy, *others):
        cores[i].wait_recv()
        q[i] = pair_sum(i, *others).astype(BF16)
        copy.start()

    far_pair = ((y + 2) % 4) // 2
    per_pair = row_blocks // 4
    spread(1, 0, row_blocks)
    collect(1)
    hand_on(2)
    send_terms(4)
    send_terms(5)
    start_back(1)
    for h in (0, 1):
        grad_rows(far_pair * per_pair + h * 2 * per_pair, per_pair)
    cores[0].start()
    cores[1].start()
    hand_on(3)
    for h in (0, 1):
        grad_rows((1 - far_pair) * per_pair + h * 2 * per_pair, per_pair)
    for i in (4, 2, 3, 5, 6, 7):
        cores[i].start()
    for i in range(2):
        send_sum(i, far[i])
    end_back(0)
    finish_half(0)
    send_sum(4, near[2])
    hand_on(4)
    send_terms(6)
    back_sums[1].share()
    hand_on(5)
    send_terms(7)
    far[0].wait_recv()
    send_sum(2, near[0], ry2.at[0])
    send_sum(3, near[1])
    far[1].wait_recv()
    send_sum(5, near[3], ry2.at[1])
    hand_on(6)
    end_back(1)
    product = (
        lax.dot_general(
            tokv[...].reshape(rows, width), backv[...], (((0,), (0,)), ((), ())), preferred_element_type=F32
        )
        * norm_scale
    )
    grow = gright.shape[0]
    for k in range(SEQS):
        grsend[k // 2, k % 2] = product[k * grow : (k + 1) * grow, :].astype(BF16)
    pair = remote(grsend.at[:, 1 - core], grpair, gps, gpr, p, sibling)
    pair.start()
    place_ = half * 4 + y
    rights = []
    for k in range(1, SEQS // 2):
        there = (place_ + k) % (SEQS // 2)
        rights.append(
            remote(grsum.at[there], grrecv.at[k - 1], gs.at[k - 1], gr.at[k - 1], p, there * 2 + core)
        )
    hand_on(7)
    pair.wait_recv()
    grsum[...] = (grsend[:, core].astype(F32) + grpair[...].astype(F32)).astype(BF16)
    for copy in rights:
        copy.start()
    finish_half(1)
    for copy in (near[0], near[2], cores[6]):
        copy.wait_recv()
    zsend[...] = pair_sum(6, ry1.at[0], ry1.at[2]).astype(BF16)
    cross = remote(zsend, zrecv, hs, hr, p, other_half)
    cross.start()
    for copy in (near[1], near[3], cores[7]):
        copy.wait_recv()
    total = grsend[place_, core].astype(F32) + grpair[place_].astype(F32)
    for k, copy in enumerate(rights):
        copy.wait_recv()
        total = total + grrecv[k].astype(F32)
    gright[...] = total
    cross.wait_recv()
    grad[...] = pair_sum(7, ry1.at[1], ry1.at[3], zrecv)
    for copy in regroup:
        copy.wait_recv()
    latent.drain()
    for each in back_sums:
        each.drain()
    for copy in own + passed + across + first + second + upward + cores + far + near + rights + regroup + [cross, pair]:
        copy.wait_send()
    for copy in act_outs:
        copy.wait()


def chain_links(pattern, blocks):
    count = pattern.shape[0]
    total = 2 * count + blocks
    place = lax.rem(pattern[:, 0], blocks)
    r = lax.broadcasted_iota(jnp.int32, (total, count), 0)
    g = lax.broadcasted_iota(jnp.int32, (total, count), 1)
    across = jnp.broadcast_to(place[None, :], (total, count))
    down = jnp.broadcast_to(jnp.pad(place, (0, total - count))[:, None], (total, count))
    is_row, is_place = r < count, r < count + blocks
    linked = jnp.where(is_row, (down == across) & (g < r), across == r - count)
    found = jnp.where(linked, g + 1, 0)
    own = jnp.where(g == r - count - blocks, across, 0)
    return jnp.max(jnp.where(is_place, found, own), axis=1)


def fused(tokens, weights, left, right, pattern, cotangent, norm_scale):
    rows, width = tokens.shape
    out_rows, wide = weights.shape
    rank = left.shape[1]
    slab = rows // FEATS
    row_blocks, blocks = out_rows // BLK, width // BLK
    piece, grow = out_rows // SEQS, width // SEQS
    all_wide = wide + rank
    any_spec = pl.BlockSpec(memory_space=pl.ANY)
    vmem_spec = pl.BlockSpec(memory_space=pltpu.VMEM)
    smem_spec = pl.BlockSpec(memory_space=pltpu.SMEM)
    dma = pltpu.SemaphoreType.DMA
    d8, d7, d4, d2, d27 = dma((8,)), dma((7,)), dma((4,)), dma((2,)), dma((2, 7))
    small = slab // 2
    half = pltpu.VMEM((FEATS, small, width), BF16)
    whole = pltpu.VMEM((rows, width), BF16)
    slabs, slabs7 = pltpu.VMEM((FEATS, slab, rank), BF16), pltpu.VMEM((FEATS - 1, slab, rank), BF16)
    flat = pltpu.VMEM((rows, rank), BF16)
    return pl.pallas_call(
        functools.partial(kernel, norm_scale),
        out_shape=(
            jax.ShapeDtypeStruct((FEATS, 2, slab // 2, out_rows), BF16),
            jax.ShapeDtypeStruct((FEATS, slab, width), BF16),
            jax.ShapeDtypeStruct((piece, all_wide), F32),
            jax.ShapeDtypeStruct((grow, rank), F32),
        ),
        in_specs=[smem_spec, any_spec, any_spec, any_spec, any_spec, vmem_spec],
        out_specs=(any_spec, vmem_spec, vmem_spec, vmem_spec),
        scratch_shapes=[
            pltpu.VMEM((blocks, rows, wide), BF16),
            pltpu.VMEM((2, FEATS, small, width), BF16), half, half, half, half, half, half,
            pltpu.VMEM((out_rows, wide), BF16), pltpu.VMEM((out_rows, rank), BF16),
            pltpu.VMEM((rows, out_rows), BF16), pltpu.VMEM((rows, out_rows), BF16),
            pltpu.VMEM((row_blocks + 1, rows // 2, wide), F32),
            pltpu.VMEM((LEVELS, rows, width), BF16),
            pltpu.VMEM((out_rows, all_wide), BF16),
            pltpu.VMEM((FEATS, slab, rank), F32), slabs, slabs7, slabs, flat,
            pltpu.VMEM((2, FEATS, small, rank), F32), pltpu.VMEM((2, FEATS, small, rank), BF16),
            pltpu.VMEM((2, FEATS - 1, small, rank), BF16), pltpu.VMEM((2, FEATS, small, rank), BF16), flat,
            whole, whole, whole,
            pltpu.VMEM((8, piece, all_wide), BF16), pltpu.VMEM((6, piece, all_wide), BF16),
            pltpu.VMEM((2, piece, all_wide), BF16), pltpu.VMEM((4, piece, all_wide), BF16),
            pltpu.VMEM((piece, all_wide), BF16), pltpu.VMEM((piece, all_wide), BF16),
            pltpu.VMEM((SEQS // 2, 2, grow, rank), BF16), pltpu.VMEM((SEQS // 2, grow, rank), BF16),
            pltpu.VMEM((SEQS // 2, grow, rank), BF16), pltpu.VMEM((SEQS // 2 - 1, grow, rank), BF16),
            dma((20,)), d8, d8, d8, d8, d8, d8, d7, d7, d7, d7, d27, d27, d27, d27,
            d8, d8, d8, d8, d8, d8, d27, d27, d8, d8, d2, d2, d4, d4, dma, dma, dma, dma, d7, d7, dma((16,)),
        ],
        compiler_params=pltpu.CompilerParams(collective_id=0, has_side_effects=True, vmem_limit_bytes=VMEM_LIMIT),
    )(
        chain_links(pattern, blocks),
        tokens.reshape(FEATS, 2, slab // 2, width),
        weights,
        left,
        cotangent.reshape(FEATS, 2, slab // 2, out_rows),
        right,
    )


def place_kernel(wide, act, a2a, grad, gright, act_o, gin_o, gb_o, gl_o, gr_o, actv, a2av, gradv, grv, in_sem, out_sem):
    parts = 4
    step = act.shape[0] // parts
    width = a2a.shape[2]
    rows = [pl.ds(i * step, step) for i in range(parts)]
    moves = [(act.at[r, :], actv.at[r, :], [(actv.at[r, :], act_o.at[r, :])]) for r in rows]
    moves.append(
        (grad, gradv, [(gradv.at[:, pl.ds(0, wide)], gb_o), (gradv.at[:, pl.ds(wide, gradv.shape[1] - wide)], gl_o)])
    )
    moves.append((gright, grv, [(grv, gr_o)]))
    moves += [
        (a2a.at[c], a2av.at[c], [(a2av.at[c], gin_o.at[:, pl.ds(c * width, width)])]) for c in range(a2a.shape[0])
    ]
    ins = [pltpu.make_async_copy(src, mid, in_sem.at[i]) for i, (src, mid, _) in enumerate(moves)]
    for copy in ins:
        copy.start()
    outs = []
    for copy, (_, _, after) in zip(ins, moves):
        copy.wait()
        for src, dst in after:
            outs.append(pltpu.make_async_copy(src, dst, out_sem.at[len(outs)]))
            outs[-1].start()
    for copy in outs:
        copy.wait()


def place(act, a2a, grad, gright, wide):
    any_spec = pl.BlockSpec(memory_space=pl.ANY)
    feats, slab, width = a2a.shape
    piece, all_wide = grad.shape
    dma = pltpu.SemaphoreType.DMA
    return pl.pallas_call(
        functools.partial(place_kernel, wide),
        out_shape=(
            jax.ShapeDtypeStruct(act.shape, BF16),
            jax.ShapeDtypeStruct((slab, feats * width), BF16),
            jax.ShapeDtypeStruct((piece, wide), F32),
            jax.ShapeDtypeStruct((piece, all_wide - wide), F32),
            jax.ShapeDtypeStruct(gright.shape, F32),
        ),
        in_specs=[any_spec] * 4,
        out_specs=(any_spec,) * 5,
        scratch_shapes=[
            pltpu.VMEM(act.shape, BF16), pltpu.VMEM(a2a.shape, BF16),
            pltpu.VMEM(grad.shape, F32), pltpu.VMEM(gright.shape, F32),
            dma((14,)), dma((15,)),
        ],
        compiler_params=pltpu.CompilerParams(vmem_limit_bytes=VMEM_LIMIT),
    )(act, a2a, grad, gright)


def local(tokens, block_weights, left_factor, right_factor, pattern, cotangent):
    norm_scale = 1.0 / math.sqrt(tokens.shape[0] * lax.axis_size("seq"))
    act, a2a, grad, gright = fused(
        tokens, block_weights, left_factor, right_factor, pattern, cotangent, norm_scale
    )
    activated, grad_input, grad_blocks, grad_left, grad_right = place(
        act.reshape(cotangent.shape), a2a, grad, gright, block_weights.shape[1]
    )
    return activated, grad_input[None], grad_blocks, grad_left, grad_right


def solution(mesh):
    in_specs = (
        P("seq", "feat"),
        P("feat", None),
        P("feat", None),
        P("feat", None),
        P("feat", None),
        P("seq", "feat"),
    )
    out_specs = (
        P("seq", "feat"),
        P("seq", "feat", None),
        P(("feat", "seq"), None),
        P(("feat", "seq"), None),
        P(("feat", "seq"), None),
    )
    return jax.shard_map(local, mesh=mesh, in_specs=in_specs, out_specs=out_specs, check_vma=False)
```

```python
import functools
import math

import jax
import jax.numpy as jnp
import numpy as np
from jax import lax
from jax.experimental import pallas as pl
from jax.experimental.pallas import tpu as pltpu
from jax.sharding import PartitionSpec as P

BLK = 128
LEVELS = 4
FEATS = 8
SEQS = 16
UNROLL = 4
MESH = pl.DeviceIdType.MESH
F32 = jnp.float32
BF16 = jnp.bfloat16
VMEM_LIMIT = 67043328


def remote(src, dst, send_sem, recv_sem, feat, seq):
    return pltpu.make_async_remote_copy(
        src_ref=src,
        dst_ref=dst,
        send_sem=send_sem,
        recv_sem=recv_sem,
        device_id=(feat, seq),
        device_id_type=MESH,
    )


def greet(devices):
    barrier = pltpu.get_barrier_semaphore()
    for feat, seq in devices:
        pl.semaphore_signal(barrier, inc=1, device_id=(feat, seq), device_id_type=MESH)
    return lambda: pl.semaphore_wait(barrier, len(devices))


class FeatSum:
    def __init__(self, p, s, part, outgoing, landed, shared, sems):
        rs_send, rs_recv, ag_send, ag_recv = sems
        self.p, self.part, self.outgoing, self.landed, self.shared = p, part, outgoing, landed, shared
        self.rs, self.ag = [], []
        for k in range(1, FEATS):
            there = (p + k) % FEATS
            self.rs.append(
                remote(outgoing.at[there], landed.at[k - 1], rs_send.at[k - 1], rs_recv.at[k - 1], there, s)
            )
            self.ag.append(remote(shared.at[p], shared.at[p], ag_send.at[k - 1], ag_recv.at[k - 1], there, s))

    def cast(self):
        self.outgoing[...] = self.part[...].astype(BF16)

    def send(self):
        for copy in self.rs:
            copy.start()

    def share(self):
        total = self.part[self.p]
        for k, copy in enumerate(self.rs):
            copy.wait_recv()
            total = total + self.landed[k].astype(F32)
        self.shared[self.p] = total.astype(BF16)
        for copy in self.ag:
            copy.start()

    def finish(self):
        for copy in self.ag:
            copy.wait_recv()

    def drain(self):
        for copy in self.rs + self.ag:
            copy.wait_send()


def loop(first, count, fn):
    def body(i, carry):
        for u in range(UNROLL):
            fn(first + i * UNROLL + u)
        return carry

    lax.fori_loop(0, count // UNROLL, body, 0)
    for u in range(count % UNROLL):
        fn(first + count - count % UNROLL + u)


def block_of(f):
    start = f * BLK
    return pl.ds(start if isinstance(start, int) else pl.multiple_of(start, BLK), BLK)


def kernel(norm_scale, *refs):
    (links, tok, w_hbm, left_hbm, cot_hbm, right) = refs[:6]
    (act_hbm, a2a, grad, gright) = refs[6:10]
    (
        xall, tokv, x1a, x1b, x2a, x2b, x3a, x3b, wv, leftv, gp, actv, sums, terms, grads,
        part, outgoing, landed, shared, lat, backp, backo, backl, backs, backv, rx1, rx2, rz,
        crecv, q, ry2, ry1, zsend, zrecv, grsend, grpair, grsum, grrecv,
    ) = refs[10:48]
    (
        lsem, x_send, x_recv, f_send, f_recv, z_send, z_recv, rs_send, rs_recv, ag_send, ag_recv,
        rs_send2, rs_recv2, ag_send2, ag_recv2, x1s, x1r, x2s, x2r, zs, zr, as_, ar,
        cs, cr, y2s, y2r, y1s, y1r, hs, hr, gps, gpr, gs, gr, act_sem,
    ) = refs[48:]
    p, s = lax.axis_index("feat"), lax.axis_index("seq")
    x, z = p // 2, p % 2
    side, back, up = 2 * (x + 1 - 2 * (x % 2)) + z, 2 * (3 - x) + z, 2 * x + 1 - z
    core, y, half = s % 2, (s // 2) % 4, s // 8
    slab, rank = part.shape[1], part.shape[2]
    small, width = tokv.shape[2], tokv.shape[3]
    rows = FEATS * slab
    mid_rows = rows // 2
    blocks = width // BLK
    row_blocks = wv.shape[0] // BLK
    wide = LEVELS * BLK
    piece = crecv.shape[1]

    def part_of(ref, h, c):
        return ref.at[pl.ds(h * mid_rows + c * small, small), :]

    tok_loads = [pltpu.make_async_copy(tok.at[:, h], tokv.at[h], lsem.at[h]) for h in range(2)]
    loads = [pltpu.make_async_copy(w_hbm, wv, lsem.at[2]), pltpu.make_async_copy(left_hbm, leftv, lsem.at[3])]
    for h in range(2):
        for c in range(FEATS):
            loads.append(
                pltpu.make_async_copy(cot_hbm.at[c, h], part_of(gp, h, c), lsem.at[4 + h * FEATS + c])
            )
    for copy in tok_loads + loads:
        copy.start()
    all_here = greet([((p + k) % FEATS, s) for k in range(1, FEATS)] + [(p, (s + k) % SEQS) for k in range(1, SEQS)])

    def chunk(pair, c):
        return pair[c // 4].at[pl.ds((c % 4) * 2, 2)]

    def own_chunk(c):
        return tok.at[pl.ds((c % 4) * 2, 2), c // 4]

    def at(ref, c):
        return ref.at[pl.ds(c * slab, slab), :]

    own = [remote(own_chunk(c), chunk((x2a, x2b), c), x_send.at[c], x_recv.at[c], side, s) for c in range(FEATS)]
    passed = [
        remote(chunk((x2a, x2b), c), chunk((x1a, x1b), c), f_send.at[c], f_recv.at[c], back, s) for c in range(FEATS)
    ]
    across = [remote(own_chunk(c), chunk((x3a, x3b), c), z_send.at[c], z_recv.at[c], up, s) for c in range(FEATS)]
    latent = FeatSum(p, s, part, outgoing, landed, shared, (rs_send, rs_recv, ag_send, ag_recv))
    for copy in tok_loads:
        copy.wait()
    for c in range(FEATS):
        mine = tokv[c // 4, (c % 4) * 2 : (c % 4) * 2 + 2].reshape(slab, width)
        part[c] = jnp.dot(mine, right[...], preferred_element_type=F32)
    latent.cast()
    all_here()
    latent.send()

    def send_own(c):
        own[c].start()
        across[c].start()

    send_own(0)

    sums[0] = jnp.zeros(sums.shape[1:], F32)

    def relay(c):
        own[c].wait_recv()
        passed[c].start()

    latent.share()
    send_own(1)
    send_own(2)
    relay(0)
    send_own(3)
    relay(1)
    send_own(4)
    relay(2)
    send_own(5)
    send_own(6)
    relay(3)
    send_own(7)
    relay(4)

    def halves(h):
        return slice(h * mid_rows, (h + 1) * mid_rows)

    def repack(h):
        for j, source in enumerate((tokv.at[h], (x1a, x1b)[h], (x2a, x2b)[h], (x3a, x3b)[h])):
            for b in range(blocks):
                block = source[:, :, b * BLK : (b + 1) * BLK].reshape(mid_rows, BLK)
                xall[b, halves(h), j * BLK : (j + 1) * BLK] = block

    def picked(here, f):
        return jnp.concatenate([xall[links[row_blocks + blocks + f], here, :], lat[here, :]], axis=1)

    curve = math.sqrt(2.0 / math.pi)

    def forward(h, first, count):
        here = slice(h * mid_rows, (h + 1) * mid_rows)

        def one(f):
            fr = block_of(f)
            wl = jnp.concatenate([wv[fr, :], leftv[fr, :]], axis=1)
            pre = lax.dot_general(picked(halves(h), f), wl, (((1,), (1,)), ((), ())), preferred_element_type=F32)
            square = pre * pre
            th = jnp.tanh(curve * (pre + 0.044715 * (square * pre)))
            cdf = 0.5 + 0.5 * th
            actv[here, fr] = (pre * cdf).astype(BF16)
            slope = cdf + (0.5 * curve) * pre * (1.0 - th * th) * (1.0 + (3.0 * 0.044715) * square)
            gp[here, fr] = (gp[here, fr].astype(F32) * slope).astype(BF16)

        loop(first, count, one)

    def spread(h, begin, count):
        here = slice(h * mid_rows, (h + 1) * mid_rows)

        def one(f):
            fr = block_of(f)
            sums[f + 1] = sums[links[f]] + jnp.dot(gp[here, fr], wv[fr, :], preferred_element_type=F32)

        loop(begin, count, one)

    def collect(h):
        here = slice(h * mid_rows, (h + 1) * mid_rows)
        for b in range(blocks):
            total = sums[links[row_blocks + b]].astype(BF16)
            for j in range(LEVELS):
                terms[j, here, b * BLK : (b + 1) * BLK] = total[:, j * BLK : (j + 1) * BLK]

    first = [remote(at(terms.at[1], c), at(rx1, c), x1s.at[c], x1r.at[c], back, s) for c in range(FEATS)]
    second = [remote(at(rx1, c), at(rx2, c), x2s.at[c], x2r.at[c], side, s) for c in range(FEATS)]
    upward = [remote(at(terms.at[3], c), at(rz, c), zs.at[c], zr.at[c], up, s) for c in range(FEATS)]

    def send_terms(c):
        first[c].start()
        upward[c].start()

    def hand_on(c):
        here = slice(c * slab, (c + 1) * slab)
        first[c].wait_recv()
        rx1[here, :] = (terms[2, here, :].astype(F32) + rx1[here, :].astype(F32)).astype(BF16)
        second[c].start()

    def back_sum_of(h):
        return FeatSum(
            p, s, backp.at[h], backo.at[h], backl.at[h], backs.at[h],
            (rs_send2.at[h], rs_recv2.at[h], ag_send2.at[h], ag_recv2.at[h]),
        )

    back_sums = [back_sum_of(0), back_sum_of(1)]

    def start_back(h):
        for c in range(FEATS):
            here = slice(h * mid_rows + c * small, h * mid_rows + (c + 1) * small)
            if c % 4 == 0:
                wider = slice(h * mid_rows + c * small, h * mid_rows + (c + 4) * small)
                four = jnp.dot(gp[wider, :], leftv[...], preferred_element_type=F32)
            backp[h, c] = four[(c % 4) * small : (c % 4 + 1) * small, :]
        back_sums[h].cast()
        back_sums[h].send()

    def end_back(h):
        back_sums[h].finish()
        for c in range(FEATS):
            backv[h * mid_rows + c * small : h * mid_rows + (c + 1) * small, :] = backs[h, c]

    regroup = []
    for h in range(2):
        for k in range(1, FEATS):
            there = (p + k) % FEATS
            src = terms.at[0, pl.ds(pl.multiple_of(h * mid_rows + there * small, small), small), :]
            dst = a2a.at[p, pl.ds(h * small, small), :]
            regroup.append(remote(src, dst, as_.at[h, k - 1], ar.at[h, k - 1], there, s))

    def finish_half(h):
        lows = lax.dot_general(
            backv[halves(h), :], right[...], (((1,), (1,)), ((), ())), preferred_element_type=F32
        )
        for c in range(h * 4, h * 4 + 4):
            here = slice(c * slab, (c + 1) * slab)
            low = lows[(c % 4) * slab : (c % 4 + 1) * slab, :]
            second[c].wait_recv()
            upward[c].wait_recv()
            terms[0, here, :] = (
                low + terms[0, here, :].astype(F32) + rx2[here, :].astype(F32) + rz[here, :].astype(F32)
            ).astype(BF16)
        for copy in regroup[h * (FEATS - 1) : (h + 1) * (FEATS - 1)]:
            copy.start()
        a2a[p, h * small : (h + 1) * small, :] = terms[
            0, pl.ds(pl.multiple_of(h * mid_rows + p * small, small), small), :
        ]

    latent.finish()
    for c in range(FEATS):
        lat[c * slab : (c + 1) * slab, :] = shared[c]
    for c in range(4):
        passed[c].wait_recv()
        across[c].wait_recv()
    for copy in loads:
        copy.wait()
    repack(0)
    forward(0, 0, 12)
    relay(5)
    forward(0, 12, row_blocks - 12)
    relay(6)
    spread(0, 0, row_blocks // 2)
    relay(7)
    spread(0, row_blocks // 2, row_blocks - row_blocks // 2)
    collect(0)
    start_back(0)
    send_terms(0)
    send_terms(1)
    for c in range(4, FEATS):
        passed[c].wait_recv()
        across[c].wait_recv()
    repack(1)
    forward(1, 0, 12)
    hand_on(0)
    send_terms(2)
    back_sums[0].share()
    forward(1, 12, row_blocks - 12)
    hand_on(1)
    send_terms(3)
    act_outs = []
    for h in range(2):
        for c in range(FEATS):
            act_outs.append(
                pltpu.make_async_copy(part_of(actv, h, c), act_hbm.at[c, h], act_sem.at[h * FEATS + c])
            )
            act_outs[-1].start()

    def seq_at(half_, y_, core_):
        return half_ * 8 + y_ * 2 + core_

    def grad_rows(first_block, count):
        def one(f):
            fr = block_of(f)
            xl = picked(slice(0, rows), f)
            grads[fr, :] = (
                lax.dot_general(gp[:, fr], xl, (((0,), (0,)), ((), ())), preferred_element_type=F32) * norm_scale
            ).astype(BF16)

        loop(first_block, count, one)

    slots = [(dy, h) for dy in (2, 1, 3, 0) for h in (0, 1)]

    def rows_of(dy, h, core_):
        there = half if h == 1 else 1 - half
        return pl.ds(pl.multiple_of(seq_at(there, (y + dy) % 4, core_) * piece, 32), piece)

    sibling = seq_at(half, y, 1 - core)
    up_y, down_y = seq_at(half, (y + 1) % 4, core), seq_at(half, (y + 3) % 4, core)
    other_half = seq_at(1 - half, y, core)
    cores = [
        remote(grads.at[rows_of(dy, h, 1 - core), :], crecv.at[i], cs.at[i], cr.at[i], p, sibling)
        for i, (dy, h) in enumerate(slots)
    ]
    far = [
        remote(q.at[0], ry2.at[0], y2s.at[0], y2r.at[0], p, up_y),
        remote(q.at[1], ry2.at[1], y2s.at[1], y2r.at[1], p, down_y),
    ]
    near = [remote(q.at[2 + i], ry1.at[i], y1s.at[i], y1r.at[i], p, up_y if i < 2 else down_y) for i in range(4)]

    def pair_sum(i, *others):
        dy, h = slots[i]
        total = grads[rows_of(dy, h, core), :].astype(F32) + crecv[i].astype(F32)
        for other in others:
            total = total + other[...].astype(F32)
        return total

    def send_sum(i, copy, *others):
        cores[i].wait_recv()
        q[i] = pair_sum(i, *others).astype(BF16)
        copy.start()

    far_pair = ((y + 2) % 4) // 2
    per_pair = row_blocks // 4
    for h in (0, 1):
        grad_rows(far_pair * per_pair + h * 2 * per_pair, per_pair)
    cores[0].start()
    cores[1].start()
    spread(1, 0, row_blocks // 2)
    for i in range(2):
        send_sum(i, far[i])
    hand_on(2)
    spread(1, row_blocks // 2, row_blocks - row_blocks // 2)
    collect(1)
    start_back(1)
    send_terms(4)
    send_terms(5)
    hand_on(3)
    send_terms(6)
    for h in (0, 1):
        grad_rows((1 - far_pair) * per_pair + h * 2 * per_pair, per_pair)
    for i in (4, 2, 3, 5, 6, 7):
        cores[i].start()
    hand_on(4)
    send_terms(7)
    end_back(0)
    finish_half(0)
    send_sum(4, near[2])
    far[0].wait_recv()
    send_sum(2, near[0], ry2.at[0])
    send_sum(3, near[1])
    far[1].wait_recv()
    send_sum(5, near[3], ry2.at[1])
    hand_on(5)
    back_sums[1].share()
    hand_on(6)
    end_back(1)
    product = (
        lax.dot_general(
            tokv[...].reshape(rows, width), backv[...], (((0,), (0,)), ((), ())), preferred_element_type=F32
        )
        * norm_scale
    )
    grow = gright.shape[0]
    for k in range(SEQS):
        grsend[k // 2, k % 2] = product[k * grow : (k + 1) * grow, :].astype(BF16)
    pair = remote(grsend.at[:, 1 - core], grpair, gps, gpr, p, sibling)
    pair.start()
    place_ = half * 4 + y
    rights = []
    for k in range(1, SEQS // 2):
        there = (place_ + k) % (SEQS // 2)
        rights.append(
            remote(grsum.at[there], grrecv.at[k - 1], gs.at[k - 1], gr.at[k - 1], p, there * 2 + core)
        )
    hand_on(7)
    pair.wait_recv()
    grsum[...] = (grsend[:, core].astype(F32) + grpair[...].astype(F32)).astype(BF16)
    for copy in rights:
        copy.start()
    for copy in (near[0], near[2], cores[6]):
        copy.wait_recv()
    zsend[...] = pair_sum(6, ry1.at[0], ry1.at[2]).astype(BF16)
    cross = remote(zsend, zrecv, hs, hr, p, other_half)
    cross.start()
    finish_half(1)
    for copy in (near[1], near[3], cores[7]):
        copy.wait_recv()
    total = grsend[place_, core].astype(F32) + grpair[place_].astype(F32)
    for k, copy in enumerate(rights):
        copy.wait_recv()
        total = total + grrecv[k].astype(F32)
    gright[...] = total
    cross.wait_recv()
    grad[...] = pair_sum(7, ry1.at[1], ry1.at[3], zrecv)
    for copy in regroup:
        copy.wait_recv()
    latent.drain()
    for each in back_sums:
        each.drain()
    for copy in own + passed + across + first + second + upward + cores + far + near + rights + regroup + [cross, pair]:
        copy.wait_send()
    for copy in act_outs:
        copy.wait()


def chain_links(pattern, blocks):
    count = pattern.shape[0]
    total = 2 * count + blocks
    place = lax.rem(pattern[:, 0], blocks)
    r, g = np.arange(total)[:, None], np.arange(count)[None, :]
    across = jnp.broadcast_to(place[None, :], (total, count))
    down = jnp.broadcast_to(jnp.pad(place, (0, total - count))[:, None], (total, count))
    linked = jnp.where(r < count, (down == across) & (g < r), across == np.broadcast_to(r - count, (total, count)))
    found = jnp.where(linked, np.int32(g + 1), 0)
    own = jnp.where(g == r - count - blocks, across, 0)
    return jnp.max(jnp.where(r < count + blocks, found, own), axis=1).astype(jnp.int32)


def fused(tokens, weights, left, right, pattern, cotangent, norm_scale):
    rows, width = tokens.shape
    out_rows, wide = weights.shape
    rank = left.shape[1]
    slab = rows // FEATS
    row_blocks, blocks = out_rows // BLK, width // BLK
    piece, grow = out_rows // SEQS, width // SEQS
    all_wide = wide + rank
    any_spec = pl.BlockSpec(memory_space=pl.ANY)
    vmem_spec = pl.BlockSpec(memory_space=pltpu.VMEM)
    smem_spec = pl.BlockSpec(memory_space=pltpu.SMEM)
    dma = pltpu.SemaphoreType.DMA
    d8, d7, d4, d2, d27 = dma((8,)), dma((7,)), dma((4,)), dma((2,)), dma((2, 7))
    small = slab // 2
    half = pltpu.VMEM((FEATS, small, width), BF16)
    whole = pltpu.VMEM((rows, width), BF16)
    slabs, slabs7 = pltpu.VMEM((FEATS, slab, rank), BF16), pltpu.VMEM((FEATS - 1, slab, rank), BF16)
    flat = pltpu.VMEM((rows, rank), BF16)
    return pl.pallas_call(
        functools.partial(kernel, norm_scale),
        out_shape=(
            jax.ShapeDtypeStruct((FEATS, 2, slab // 2, out_rows), BF16),
            jax.ShapeDtypeStruct((FEATS, slab, width), BF16),
            jax.ShapeDtypeStruct((piece, all_wide), F32),
            jax.ShapeDtypeStruct((grow, rank), F32),
        ),
        in_specs=[smem_spec, any_spec, any_spec, any_spec, any_spec, vmem_spec],
        out_specs=(any_spec, vmem_spec, vmem_spec, vmem_spec),
        scratch_shapes=[
            pltpu.VMEM((blocks, rows, wide), BF16),
            pltpu.VMEM((2, FEATS, small, width), BF16), half, half, half, half, half, half,
            pltpu.VMEM((out_rows, wide), BF16), pltpu.VMEM((out_rows, rank), BF16),
            pltpu.VMEM((rows, out_rows), BF16), pltpu.VMEM((rows, out_rows), BF16),
            pltpu.VMEM((row_blocks + 1, rows // 2, wide), F32),
            pltpu.VMEM((LEVELS, rows, width), BF16),
            pltpu.VMEM((out_rows, all_wide), BF16),
            pltpu.VMEM((FEATS, slab, rank), F32), slabs, slabs7, slabs, flat,
            pltpu.VMEM((2, FEATS, small, rank), F32), pltpu.VMEM((2, FEATS, small, rank), BF16),
            pltpu.VMEM((2, FEATS - 1, small, rank), BF16), pltpu.VMEM((2, FEATS, small, rank), BF16), flat,
            whole, whole, whole,
            pltpu.VMEM((8, piece, all_wide), BF16), pltpu.VMEM((6, piece, all_wide), BF16),
            pltpu.VMEM((2, piece, all_wide), BF16), pltpu.VMEM((4, piece, all_wide), BF16),
            pltpu.VMEM((piece, all_wide), BF16), pltpu.VMEM((piece, all_wide), BF16),
            pltpu.VMEM((SEQS // 2, 2, grow, rank), BF16), pltpu.VMEM((SEQS // 2, grow, rank), BF16),
            pltpu.VMEM((SEQS // 2, grow, rank), BF16), pltpu.VMEM((SEQS // 2 - 1, grow, rank), BF16),
            dma((20,)), d8, d8, d8, d8, d8, d8, d7, d7, d7, d7, d27, d27, d27, d27,
            d8, d8, d8, d8, d8, d8, d27, d27, d8, d8, d2, d2, d4, d4, dma, dma, dma, dma, d7, d7, dma((16,)),
        ],
        compiler_params=pltpu.CompilerParams(collective_id=0, has_side_effects=True, vmem_limit_bytes=VMEM_LIMIT),
    )(
        chain_links(pattern, blocks),
        tokens.reshape(FEATS, 2, slab // 2, width),
        weights,
        left,
        cotangent.reshape(FEATS, 2, slab // 2, out_rows),
        right,
    )


def place_kernel(wide, act, a2a, grad, gright, act_o, gin_o, gb_o, gl_o, gr_o, actv, a2av, gradv, grv, in_sem, out_sem):
    parts = 4
    step = act.shape[0] // parts
    width = a2a.shape[2]
    rows = [pl.ds(i * step, step) for i in range(parts)]
    moves = [(act.at[r, :], actv.at[r, :], [(actv.at[r, :], act_o.at[r, :])]) for r in rows]
    moves.append(
        (grad, gradv, [(gradv.at[:, pl.ds(0, wide)], gb_o), (gradv.at[:, pl.ds(wide, gradv.shape[1] - wide)], gl_o)])
    )
    moves.append((gright, grv, [(grv, gr_o)]))
    moves += [
        (a2a.at[c], a2av.at[c], [(a2av.at[c], gin_o.at[:, pl.ds(c * width, width)])]) for c in range(a2a.shape[0])
    ]
    ins = [pltpu.make_async_copy(src, mid, in_sem.at[i]) for i, (src, mid, _) in enumerate(moves)]
    for copy in ins:
        copy.start()
    outs = []
    for copy, (_, _, after) in zip(ins, moves):
        copy.wait()
        for src, dst in after:
            outs.append(pltpu.make_async_copy(src, dst, out_sem.at[len(outs)]))
            outs[-1].start()
    for copy in outs:
        copy.wait()


def place(act, a2a, grad, gright, wide):
    any_spec = pl.BlockSpec(memory_space=pl.ANY)
    feats, slab, width = a2a.shape
    piece, all_wide = grad.shape
    dma = pltpu.SemaphoreType.DMA
    return pl.pallas_call(
        functools.partial(place_kernel, wide),
        out_shape=(
            jax.ShapeDtypeStruct(act.shape, BF16),
            jax.ShapeDtypeStruct((slab, feats * width), BF16),
            jax.ShapeDtypeStruct((piece, wide), F32),
            jax.ShapeDtypeStruct((piece, all_wide - wide), F32),
            jax.ShapeDtypeStruct(gright.shape, F32),
        ),
        in_specs=[any_spec] * 4,
        out_specs=(any_spec,) * 5,
        scratch_shapes=[
            pltpu.VMEM(act.shape, BF16), pltpu.VMEM(a2a.shape, BF16),
            pltpu.VMEM(grad.shape, F32), pltpu.VMEM(gright.shape, F32),
            dma((14,)), dma((15,)),
        ],
        compiler_params=pltpu.CompilerParams(vmem_limit_bytes=VMEM_LIMIT),
    )(act, a2a, grad, gright)


def local(tokens, block_weights, left_factor, right_factor, pattern, cotangent):
    norm_scale = 1.0 / math.sqrt(tokens.shape[0] * lax.axis_size("seq"))
    act, a2a, grad, gright = fused(
        tokens, block_weights, left_factor, right_factor, pattern, cotangent, norm_scale
    )
    activated, grad_input, grad_blocks, grad_left, grad_right = place(
        act.reshape(cotangent.shape), a2a, grad, gright, block_weights.shape[1]
    )
    return activated, grad_input[None], grad_blocks, grad_left, grad_right


def solution(mesh):
    in_specs = (
        P("seq", "feat"),
        P("feat", None),
        P("feat", None),
        P("feat", None),
        P("feat", None),
        P("seq", "feat"),
    )
    out_specs = (
        P("seq", "feat"),
        P("seq", "feat", None),
        P(("feat", "seq"), None),
        P(("feat", "seq"), None),
        P(("feat", "seq"), None),
    )
    return jax.shard_map(local, mesh=mesh, in_specs=in_specs, out_specs=out_specs, check_vma=False)
```

```python
import functools
import math

import jax
import jax.numpy as jnp
import numpy as np
from jax import lax
from jax.experimental import pallas as pl
from jax.experimental.pallas import tpu as pltpu
from jax.sharding import PartitionSpec as P

BLK = 128
LEVELS = 4
FEATS = 8
SEQS = 16
UNROLL = 4
MESH = pl.DeviceIdType.MESH
F32 = jnp.float32
BF16 = jnp.bfloat16
VMEM_LIMIT = 67043328


def remote(src, dst, send_sem, recv_sem, feat, seq):
    return pltpu.make_async_remote_copy(
        src_ref=src,
        dst_ref=dst,
        send_sem=send_sem,
        recv_sem=recv_sem,
        device_id=(feat, seq),
        device_id_type=MESH,
    )


def greet(devices):
    barrier = pltpu.get_barrier_semaphore()
    for feat, seq in devices:
        pl.semaphore_signal(barrier, inc=1, device_id=(feat, seq), device_id_type=MESH)
    pl.semaphore_wait(barrier, len(devices))


class FeatSum:
    def __init__(self, p, s, part, outgoing, landed, shared, sems):
        rs_send, rs_recv, ag_send, ag_recv = sems
        self.p, self.part, self.outgoing, self.landed, self.shared = p, part, outgoing, landed, shared
        self.rs, self.ag = [], []
        for k in range(1, FEATS):
            there = (p + k) % FEATS
            self.rs.append(
                remote(outgoing.at[there], landed.at[k - 1], rs_send.at[k - 1], rs_recv.at[k - 1], there, s)
            )
            self.ag.append(remote(shared.at[p], shared.at[p], ag_send.at[k - 1], ag_recv.at[k - 1], there, s))

    def send(self):
        self.outgoing[...] = self.part[...].astype(BF16)
        for copy in self.rs:
            copy.start()

    def share(self):
        total = self.part[self.p]
        for k, copy in enumerate(self.rs):
            copy.wait_recv()
            total = total + self.landed[k].astype(F32)
        self.shared[self.p] = total.astype(BF16)
        for copy in self.ag:
            copy.start()

    def finish(self):
        for copy in self.ag:
            copy.wait_recv()

    def drain(self):
        for copy in self.rs + self.ag:
            copy.wait_send()


def loop(first, count, fn):
    def body(i, carry):
        for u in range(UNROLL):
            fn(first + i * UNROLL + u)
        return carry

    lax.fori_loop(0, count // UNROLL, body, 0)
    for u in range(count % UNROLL):
        fn(first + count - count % UNROLL + u)


def block_of(f):
    start = f * BLK
    return pl.ds(start if isinstance(start, int) else pl.multiple_of(start, BLK), BLK)


def kernel(norm_scale, *refs):
    (links, tok, w_hbm, left_hbm, cot_hbm, right) = refs[:6]
    (act_hbm, a2a, grad, gright) = refs[6:10]
    (
        xall, tokv, x1a, x1b, x2a, x2b, x3a, x3b, wv, leftv, gp, actv, sums, terms, grads,
        part, outgoing, landed, shared, lat, backp, backo, backl, backs, backv, rx1, rx2, rz,
        crecv, q, ry2, ry1, zsend, zrecv, grsend, grpair, grsum, grrecv,
    ) = refs[10:48]
    (
        lsem, x_send, x_recv, f_send, f_recv, z_send, z_recv, rs_send, rs_recv, ag_send, ag_recv,
        rs_send2, rs_recv2, ag_send2, ag_recv2, x1s, x1r, x2s, x2r, zs, zr, as_, ar,
        cs, cr, y2s, y2r, y1s, y1r, hs, hr, gps, gpr, gs, gr, act_sem,
    ) = refs[48:]
    p, s = lax.axis_index("feat"), lax.axis_index("seq")
    x, z = p // 2, p % 2
    side, back, up = 2 * (x + 1 - 2 * (x % 2)) + z, 2 * (3 - x) + z, 2 * x + 1 - z
    core, y, half = s % 2, (s // 2) % 4, s // 8
    slab, rank = part.shape[1], part.shape[2]
    small, width = tokv.shape[2], tokv.shape[3]
    rows = FEATS * slab
    mid_rows = rows // 2
    blocks = width // BLK
    row_blocks = wv.shape[0] // BLK
    wide = LEVELS * BLK
    piece = crecv.shape[1]

    def part_of(ref, h, c):
        return ref.at[pl.ds(h * mid_rows + c * small, small), :]

    tok_loads = [pltpu.make_async_copy(tok.at[:, h], tokv.at[h], lsem.at[h]) for h in range(2)]
    loads = [pltpu.make_async_copy(w_hbm, wv, lsem.at[2]), pltpu.make_async_copy(left_hbm, leftv, lsem.at[3])]
    for h in range(2):
        for c in range(FEATS):
            loads.append(
                pltpu.make_async_copy(cot_hbm.at[c, h], part_of(gp, h, c), lsem.at[4 + h * FEATS + c])
            )
    for copy in tok_loads + loads:
        copy.start()
    greet([((p + k) % FEATS, s) for k in range(1, FEATS)] + [(p, (s + k) % SEQS) for k in range(1, SEQS)])

    def chunk(pair, c):
        return pair[c // 4].at[pl.ds((c % 4) * 2, 2)]

    def own_chunk(c):
        return tok.at[pl.ds((c % 4) * 2, 2), c // 4]

    def at(ref, c):
        return ref.at[pl.ds(c * slab, slab), :]

    own = [remote(own_chunk(c), chunk((x2a, x2b), c), x_send.at[c], x_recv.at[c], side, s) for c in range(FEATS)]
    passed = [
        remote(chunk((x2a, x2b), c), chunk((x1a, x1b), c), f_send.at[c], f_recv.at[c], back, s) for c in range(FEATS)
    ]
    across = [remote(own_chunk(c), chunk((x3a, x3b), c), z_send.at[c], z_recv.at[c], up, s) for c in range(FEATS)]
    latent = FeatSum(p, s, part, outgoing, landed, shared, (rs_send, rs_recv, ag_send, ag_recv))
    own[0].start()
    across[0].start()
    for copy in tok_loads:
        copy.wait()
    for c in range(FEATS):
        mine = tokv[c // 4, (c % 4) * 2 : (c % 4) * 2 + 2].reshape(slab, width)
        part[c] = jnp.dot(mine, right[...], preferred_element_type=F32)
    latent.send()
    for c in (1,):
        own[c].start()
        across[c].start()

    sums[0] = jnp.zeros(sums.shape[1:], F32)

    def relay(c):
        own[c].wait_recv()
        passed[c].start()
        if c + 2 < FEATS:
            own[c + 2].start()
            across[c + 2].start()

    relay(0)
    latent.share()
    for c in range(1, 5):
        relay(c)

    def halves(h):
        return slice(h * mid_rows, (h + 1) * mid_rows)

    def repack(h):
        for j, source in enumerate((tokv.at[h], (x1a, x1b)[h], (x2a, x2b)[h], (x3a, x3b)[h])):
            for b in range(blocks):
                block = source[:, :, b * BLK : (b + 1) * BLK].reshape(mid_rows, BLK)
                xall[b, halves(h), j * BLK : (j + 1) * BLK] = block

    def picked(here, f):
        return jnp.concatenate([xall[links[row_blocks + blocks + f], here, :], lat[here, :]], axis=1)

    curve = math.sqrt(2.0 / math.pi)

    def forward(h, first, count):
        here = slice(h * mid_rows, (h + 1) * mid_rows)

        def one(f):
            fr = block_of(f)
            wl = jnp.concatenate([wv[fr, :], leftv[fr, :]], axis=1)
            pre = lax.dot_general(picked(halves(h), f), wl, (((1,), (1,)), ((), ())), preferred_element_type=F32)
            square = pre * pre
            th = jnp.tanh(curve * (pre + 0.044715 * (square * pre)))
            cdf = 0.5 + 0.5 * th
            actv[here, fr] = (pre * cdf).astype(BF16)
            slope = cdf + (0.5 * curve) * pre * (1.0 - th * th) * (1.0 + (3.0 * 0.044715) * square)
            gp[here, fr] = (gp[here, fr].astype(F32) * slope).astype(BF16)

        loop(first, count, one)

    def spread(h, begin, count):
        here = slice(h * mid_rows, (h + 1) * mid_rows)

        def one(f):
            fr = block_of(f)
            sums[f + 1] = sums[links[f]] + jnp.dot(gp[here, fr], wv[fr, :], preferred_element_type=F32)

        loop(begin, count, one)

    def collect(h):
        here = slice(h * mid_rows, (h + 1) * mid_rows)
        for b in range(blocks):
            total = sums[links[row_blocks + b]].astype(BF16)
            for j in range(LEVELS):
                terms[j, here, b * BLK : (b + 1) * BLK] = total[:, j * BLK : (j + 1) * BLK]

    first = [remote(at(terms.at[1], c), at(rx1, c), x1s.at[c], x1r.at[c], back, s) for c in range(FEATS)]
    second = [remote(at(rx1, c), at(rx2, c), x2s.at[c], x2r.at[c], side, s) for c in range(FEATS)]
    upward = [remote(at(terms.at[3], c), at(rz, c), zs.at[c], zr.at[c], up, s) for c in range(FEATS)]

    def send_terms(c):
        first[c].start()
        upward[c].start()

    def hand_on(c):
        here = slice(c * slab, (c + 1) * slab)
        first[c].wait_recv()
        rx1[here, :] = (terms[2, here, :].astype(F32) + rx1[here, :].astype(F32)).astype(BF16)
        second[c].start()

    def back_sum_of(h):
        return FeatSum(
            p, s, backp.at[h], backo.at[h], backl.at[h], backs.at[h],
            (rs_send2.at[h], rs_recv2.at[h], ag_send2.at[h], ag_recv2.at[h]),
        )

    back_sums = [back_sum_of(0), back_sum_of(1)]

    def start_back(h):
        for c in range(FEATS):
            here = slice(h * mid_rows + c * small, h * mid_rows + (c + 1) * small)
            if c % 4 == 0:
                wider = slice(h * mid_rows + c * small, h * mid_rows + (c + 4) * small)
                four = jnp.dot(gp[wider, :], leftv[...], preferred_element_type=F32)
            backp[h, c] = four[(c % 4) * small : (c % 4 + 1) * small, :]
        back_sums[h].send()

    def end_back(h):
        back_sums[h].finish()
        for c in range(FEATS):
            backv[h * mid_rows + c * small : h * mid_rows + (c + 1) * small, :] = backs[h, c]

    regroup = []
    for h in range(2):
        for k in range(1, FEATS):
            there = (p + k) % FEATS
            src = terms.at[0, pl.ds(pl.multiple_of(h * mid_rows + there * small, small), small), :]
            dst = a2a.at[p, pl.ds(h * small, small), :]
            regroup.append(remote(src, dst, as_.at[h, k - 1], ar.at[h, k - 1], there, s))

    def finish_half(h):
        lows = lax.dot_general(
            backv[halves(h), :], right[...], (((1,), (1,)), ((), ())), preferred_element_type=F32
        )
        for c in range(h * 4, h * 4 + 4):
            here = slice(c * slab, (c + 1) * slab)
            low = lows[(c % 4) * slab : (c % 4 + 1) * slab, :]
            second[c].wait_recv()
            upward[c].wait_recv()
            terms[0, here, :] = (
                low + terms[0, here, :].astype(F32) + rx2[here, :].astype(F32) + rz[here, :].astype(F32)
            ).astype(BF16)
        for copy in regroup[h * (FEATS - 1) : (h + 1) * (FEATS - 1)]:
            copy.start()
        a2a[p, h * small : (h + 1) * small, :] = terms[
            0, pl.ds(pl.multiple_of(h * mid_rows + p * small, small), small), :
        ]

    latent.finish()
    for c in range(FEATS):
        lat[c * slab : (c + 1) * slab, :] = shared[c]
    for c in range(4):
        passed[c].wait_recv()
        across[c].wait_recv()
    for copy in loads:
        copy.wait()
    repack(0)
    forward(0, 0, 12)
    relay(5)
    forward(0, 12, row_blocks - 12)
    relay(6)
    spread(0, 0, row_blocks // 2)
    relay(7)
    spread(0, row_blocks // 2, row_blocks - row_blocks // 2)
    collect(0)
    start_back(0)
    send_terms(0)
    send_terms(1)
    for c in range(4, FEATS):
        passed[c].wait_recv()
        across[c].wait_recv()
    repack(1)
    forward(1, 0, 12)
    hand_on(0)
    send_terms(2)
    back_sums[0].share()
    forward(1, 12, row_blocks - 12)
    hand_on(1)
    send_terms(3)
    act_outs = []
    for h in range(2):
        for c in range(FEATS):
            act_outs.append(
                pltpu.make_async_copy(part_of(actv, h, c), act_hbm.at[c, h], act_sem.at[h * FEATS + c])
            )
            act_outs[-1].start()

    def seq_at(half_, y_, core_):
        return half_ * 8 + y_ * 2 + core_

    def grad_rows(first_block, count):
        def one(f):
            fr = block_of(f)
            xl = picked(slice(0, rows), f)
            grads[fr, :] = (
                lax.dot_general(gp[:, fr], xl, (((0,), (0,)), ((), ())), preferred_element_type=F32) * norm_scale
            ).astype(BF16)

        loop(first_block, count, one)

    slots = [(dy, h) for dy in (2, 1, 3, 0) for h in (0, 1)]

    def rows_of(dy, h, core_):
        there = half if h == 1 else 1 - half
        return pl.ds(pl.multiple_of(seq_at(there, (y + dy) % 4, core_) * piece, 32), piece)

    sibling = seq_at(half, y, 1 - core)
    up_y, down_y = seq_at(half, (y + 1) % 4, core), seq_at(half, (y + 3) % 4, core)
    other_half = seq_at(1 - half, y, core)
    cores = [
        remote(grads.at[rows_of(dy, h, 1 - core), :], crecv.at[i], cs.at[i], cr.at[i], p, sibling)
        for i, (dy, h) in enumerate(slots)
    ]
    far = [
        remote(q.at[0], ry2.at[0], y2s.at[0], y2r.at[0], p, up_y),
        remote(q.at[1], ry2.at[1], y2s.at[1], y2r.at[1], p, down_y),
    ]
    near = [remote(q.at[2 + i], ry1.at[i], y1s.at[i], y1r.at[i], p, up_y if i < 2 else down_y) for i in range(4)]

    def pair_sum(i, *others):
        dy, h = slots[i]
        total = grads[rows_of(dy, h, core), :].astype(F32) + crecv[i].astype(F32)
        for other in others:
            total = total + other[...].astype(F32)
        return total

    def send_sum(i, copy, *others):
        cores[i].wait_recv()
        q[i] = pair_sum(i, *others).astype(BF16)
        copy.start()

    far_pair = ((y + 2) % 4) // 2
    per_pair = row_blocks // 4
    for h in (0, 1):
        grad_rows(far_pair * per_pair + h * 2 * per_pair, per_pair)
    cores[0].start()
    cores[1].start()
    spread(1, 0, row_blocks // 2)
    for i in range(2):
        send_sum(i, far[i])
    hand_on(2)
    spread(1, row_blocks // 2, row_blocks - row_blocks // 2)
    collect(1)
    hand_on(3)
    start_back(1)
    send_terms(4)
    send_terms(5)
    for h in (0, 1):
        grad_rows((1 - far_pair) * per_pair + h * 2 * per_pair, per_pair)
    for i in (4, 2, 3, 5, 6, 7):
        cores[i].start()
    back_sums[1].share()
    send_sum(4, near[2])
    hand_on(4)
    send_terms(6)
    far[0].wait_recv()
    send_sum(2, near[0], ry2.at[0])
    send_sum(3, near[1])
    far[1].wait_recv()
    send_sum(5, near[3], ry2.at[1])
    hand_on(5)
    send_terms(7)
    end_back(0)
    finish_half(0)
    end_back(1)
    product = (
        lax.dot_general(
            tokv[...].reshape(rows, width), backv[...], (((0,), (0,)), ((), ())), preferred_element_type=F32
        )
        * norm_scale
    )
    grow = gright.shape[0]
    for k in range(SEQS):
        grsend[k // 2, k % 2] = product[k * grow : (k + 1) * grow, :].astype(BF16)
    pair = remote(grsend.at[:, 1 - core], grpair, gps, gpr, p, sibling)
    pair.start()
    place_ = half * 4 + y
    rights = []
    for k in range(1, SEQS // 2):
        there = (place_ + k) % (SEQS // 2)
        rights.append(
            remote(grsum.at[there], grrecv.at[k - 1], gs.at[k - 1], gr.at[k - 1], p, there * 2 + core)
        )
    hand_on(6)
    pair.wait_recv()
    grsum[...] = (grsend[:, core].astype(F32) + grpair[...].astype(F32)).astype(BF16)
    for copy in rights:
        copy.start()
    for copy in (near[0], near[2], cores[6]):
        copy.wait_recv()
    zsend[...] = pair_sum(6, ry1.at[0], ry1.at[2]).astype(BF16)
    cross = remote(zsend, zrecv, hs, hr, p, other_half)
    cross.start()
    hand_on(7)
    finish_half(1)
    for copy in (near[1], near[3], cores[7]):
        copy.wait_recv()
    total = grsend[place_, core].astype(F32) + grpair[place_].astype(F32)
    for k, copy in enumerate(rights):
        copy.wait_recv()
        total = total + grrecv[k].astype(F32)
    gright[...] = total
    cross.wait_recv()
    grad[...] = pair_sum(7, ry1.at[1], ry1.at[3], zrecv)
    for copy in regroup:
        copy.wait_recv()
    latent.drain()
    for each in back_sums:
        each.drain()
    for copy in own + passed + across + first + second + upward + cores + far + near + rights + regroup + [cross, pair]:
        copy.wait_send()
    for copy in act_outs:
        copy.wait()


def chain_links(pattern, blocks):
    count = pattern.shape[0]
    total = 2 * count + blocks
    place = lax.rem(pattern[:, 0], blocks)
    r, g = np.arange(total)[:, None], np.arange(count)[None, :]
    across = jnp.broadcast_to(place[None, :], (total, count))
    down = jnp.broadcast_to(jnp.pad(place, (0, total - count))[:, None], (total, count))
    linked = jnp.where(r < count, (down == across) & (g < r), across == np.broadcast_to(r - count, (total, count)))
    found = jnp.where(linked, np.int32(g + 1), 0)
    own = jnp.where(g == r - count - blocks, across, 0)
    return jnp.max(jnp.where(r < count + blocks, found, own), axis=1).astype(jnp.int32)


def fused(tokens, weights, left, right, pattern, cotangent, norm_scale):
    rows, width = tokens.shape
    out_rows, wide = weights.shape
    rank = left.shape[1]
    slab = rows // FEATS
    row_blocks, blocks = out_rows // BLK, width // BLK
    piece, grow = out_rows // SEQS, width // SEQS
    all_wide = wide + rank
    any_spec = pl.BlockSpec(memory_space=pl.ANY)
    vmem_spec = pl.BlockSpec(memory_space=pltpu.VMEM)
    smem_spec = pl.BlockSpec(memory_space=pltpu.SMEM)
    dma = pltpu.SemaphoreType.DMA
    d8, d7, d4, d2, d27 = dma((8,)), dma((7,)), dma((4,)), dma((2,)), dma((2, 7))
    small = slab // 2
    half = pltpu.VMEM((FEATS, small, width), BF16)
    whole = pltpu.VMEM((rows, width), BF16)
    slabs, slabs7 = pltpu.VMEM((FEATS, slab, rank), BF16), pltpu.VMEM((FEATS - 1, slab, rank), BF16)
    flat = pltpu.VMEM((rows, rank), BF16)
    return pl.pallas_call(
        functools.partial(kernel, norm_scale),
        out_shape=(
            jax.ShapeDtypeStruct((FEATS, 2, slab // 2, out_rows), BF16),
            jax.ShapeDtypeStruct((FEATS, slab, width), BF16),
            jax.ShapeDtypeStruct((piece, all_wide), F32),
            jax.ShapeDtypeStruct((grow, rank), F32),
        ),
        in_specs=[smem_spec, any_spec, any_spec, any_spec, any_spec, vmem_spec],
        out_specs=(any_spec, vmem_spec, vmem_spec, vmem_spec),
        scratch_shapes=[
            pltpu.VMEM((blocks, rows, wide), BF16),
            pltpu.VMEM((2, FEATS, small, width), BF16), half, half, half, half, half, half,
            pltpu.VMEM((out_rows, wide), BF16), pltpu.VMEM((out_rows, rank), BF16),
            pltpu.VMEM((rows, out_rows), BF16), pltpu.VMEM((rows, out_rows), BF16),
            pltpu.VMEM((row_blocks + 1, rows // 2, wide), F32),
            pltpu.VMEM((LEVELS, rows, width), BF16),
            pltpu.VMEM((out_rows, all_wide), BF16),
            pltpu.VMEM((FEATS, slab, rank), F32), slabs, slabs7, slabs, flat,
            pltpu.VMEM((2, FEATS, small, rank), F32), pltpu.VMEM((2, FEATS, small, rank), BF16),
            pltpu.VMEM((2, FEATS - 1, small, rank), BF16), pltpu.VMEM((2, FEATS, small, rank), BF16), flat,
            whole, whole, whole,
            pltpu.VMEM((8, piece, all_wide), BF16), pltpu.VMEM((6, piece, all_wide), BF16),
            pltpu.VMEM((2, piece, all_wide), BF16), pltpu.VMEM((4, piece, all_wide), BF16),
            pltpu.VMEM((piece, all_wide), BF16), pltpu.VMEM((piece, all_wide), BF16),
            pltpu.VMEM((SEQS // 2, 2, grow, rank), BF16), pltpu.VMEM((SEQS // 2, grow, rank), BF16),
            pltpu.VMEM((SEQS // 2, grow, rank), BF16), pltpu.VMEM((SEQS // 2 - 1, grow, rank), BF16),
            dma((20,)), d8, d8, d8, d8, d8, d8, d7, d7, d7, d7, d27, d27, d27, d27,
            d8, d8, d8, d8, d8, d8, d27, d27, d8, d8, d2, d2, d4, d4, dma, dma, dma, dma, d7, d7, dma((16,)),
        ],
        compiler_params=pltpu.CompilerParams(collective_id=0, has_side_effects=True, vmem_limit_bytes=VMEM_LIMIT),
    )(
        chain_links(pattern, blocks),
        tokens.reshape(FEATS, 2, slab // 2, width),
        weights,
        left,
        cotangent.reshape(FEATS, 2, slab // 2, out_rows),
        right,
    )


def place_kernel(wide, act, a2a, grad, gright, act_o, gin_o, gb_o, gl_o, gr_o, actv, a2av, gradv, grv, in_sem, out_sem):
    parts = 4
    step = act.shape[0] // parts
    width = a2a.shape[2]
    rows = [pl.ds(i * step, step) for i in range(parts)]
    moves = [(act.at[r, :], actv.at[r, :], [(actv.at[r, :], act_o.at[r, :])]) for r in rows]
    moves.append(
        (grad, gradv, [(gradv.at[:, pl.ds(0, wide)], gb_o), (gradv.at[:, pl.ds(wide, gradv.shape[1] - wide)], gl_o)])
    )
    moves.append((gright, grv, [(grv, gr_o)]))
    moves += [
        (a2a.at[c], a2av.at[c], [(a2av.at[c], gin_o.at[:, pl.ds(c * width, width)])]) for c in range(a2a.shape[0])
    ]
    ins = [pltpu.make_async_copy(src, mid, in_sem.at[i]) for i, (src, mid, _) in enumerate(moves)]
    for copy in ins:
        copy.start()
    outs = []
    for copy, (_, _, after) in zip(ins, moves):
        copy.wait()
        for src, dst in after:
            outs.append(pltpu.make_async_copy(src, dst, out_sem.at[len(outs)]))
            outs[-1].start()
    for copy in outs:
        copy.wait()


def place(act, a2a, grad, gright, wide):
    any_spec = pl.BlockSpec(memory_space=pl.ANY)
    feats, slab, width = a2a.shape
    piece, all_wide = grad.shape
    dma = pltpu.SemaphoreType.DMA
    return pl.pallas_call(
        functools.partial(place_kernel, wide),
        out_shape=(
            jax.ShapeDtypeStruct(act.shape, BF16),
            jax.ShapeDtypeStruct((slab, feats * width), BF16),
            jax.ShapeDtypeStruct((piece, wide), F32),
            jax.ShapeDtypeStruct((piece, all_wide - wide), F32),
            jax.ShapeDtypeStruct(gright.shape, F32),
        ),
        in_specs=[any_spec] * 4,
        out_specs=(any_spec,) * 5,
        scratch_shapes=[
            pltpu.VMEM(act.shape, BF16), pltpu.VMEM(a2a.shape, BF16),
            pltpu.VMEM(grad.shape, F32), pltpu.VMEM(gright.shape, F32),
            dma((14,)), dma((15,)),
        ],
        compiler_params=pltpu.CompilerParams(vmem_limit_bytes=VMEM_LIMIT),
    )(act, a2a, grad, gright)


def local(tokens, block_weights, left_factor, right_factor, pattern, cotangent):
    norm_scale = 1.0 / math.sqrt(tokens.shape[0] * lax.axis_size("seq"))
    act, a2a, grad, gright = fused(
        tokens, block_weights, left_factor, right_factor, pattern, cotangent, norm_scale
    )
    activated, grad_input, grad_blocks, grad_left, grad_right = place(
        act.reshape(cotangent.shape), a2a, grad, gright, block_weights.shape[1]
    )
    return activated, grad_input[None], grad_blocks, grad_left, grad_right


def solution(mesh):
    in_specs = (
        P("seq", "feat"),
        P("feat", None),
        P("feat", None),
        P("feat", None),
        P("feat", None),
        P("seq", "feat"),
    )
    out_specs = (
        P("seq", "feat"),
        P("seq", "feat", None),
        P(("feat", "seq"), None),
        P(("feat", "seq"), None),
        P(("feat", "seq"), None),
    )
    return jax.shard_map(local, mesh=mesh, in_specs=in_specs, out_specs=out_specs, check_vma=False)
```

```python
import functools
import math

import jax
import jax.numpy as jnp
from jax import lax
from jax.experimental import pallas as pl
from jax.experimental.pallas import tpu as pltpu
from jax.sharding import PartitionSpec as P

BLK = 128
LEVELS = 4
FEATS = 8
SEQS = 16
UNROLL = 4
MESH = pl.DeviceIdType.MESH
F32 = jnp.float32
BF16 = jnp.bfloat16
VMEM_LIMIT = 67043328


def remote(src, dst, send_sem, recv_sem, feat, seq):
    return pltpu.make_async_remote_copy(
        src_ref=src,
        dst_ref=dst,
        send_sem=send_sem,
        recv_sem=recv_sem,
        device_id=(feat, seq),
        device_id_type=MESH,
    )


def greet(devices):
    barrier = pltpu.get_barrier_semaphore()
    for feat, seq in devices:
        pl.semaphore_signal(barrier, inc=1, device_id=(feat, seq), device_id_type=MESH)
    pl.semaphore_wait(barrier, len(devices))


class FeatSum:
    def __init__(self, p, s, part, outgoing, landed, shared, sems):
        rs_send, rs_recv, ag_send, ag_recv = sems
        self.p, self.part, self.outgoing, self.landed, self.shared = p, part, outgoing, landed, shared
        self.rs, self.ag = [], []
        for k in range(1, FEATS):
            there = (p + k) % FEATS
            self.rs.append(
                remote(outgoing.at[there], landed.at[k - 1], rs_send.at[k - 1], rs_recv.at[k - 1], there, s)
            )
            self.ag.append(remote(shared.at[p], shared.at[p], ag_send.at[k - 1], ag_recv.at[k - 1], there, s))

    def send(self):
        self.outgoing[...] = self.part[...].astype(BF16)
        for copy in self.rs:
            copy.start()

    def share(self):
        total = self.part[self.p]
        for k, copy in enumerate(self.rs):
            copy.wait_recv()
            total = total + self.landed[k].astype(F32)
        self.shared[self.p] = total.astype(BF16)
        for copy in self.ag:
            copy.start()

    def finish(self):
        for copy in self.ag:
            copy.wait_recv()

    def drain(self):
        for copy in self.rs + self.ag:
            copy.wait_send()


def loop(first, count, fn):
    def body(i, carry):
        for u in range(UNROLL):
            fn(first + i * UNROLL + u)
        return carry

    lax.fori_loop(0, count // UNROLL, body, 0)
    for u in range(count % UNROLL):
        fn(first + count - count % UNROLL + u)


def block_of(f):
    start = f * BLK
    return pl.ds(start if isinstance(start, int) else pl.multiple_of(start, BLK), BLK)


def kernel(norm_scale, *refs):
    (links, tok, w_hbm, left_hbm, cot_hbm, right) = refs[:6]
    (act_hbm, a2a, grad, gright) = refs[6:10]
    (
        xall, tokv, x1a, x1b, x2a, x2b, x3a, x3b, wv, leftv, gp, actv, sums, terms, grads,
        part, outgoing, landed, shared, lat, backp, backo, backl, backs, backv, rx1, rx2, rz,
        crecv, q, ry2, ry1, zsend, zrecv, grsend, grpair, grsum, grrecv,
    ) = refs[10:48]
    (
        lsem, x_send, x_recv, f_send, f_recv, z_send, z_recv, rs_send, rs_recv, ag_send, ag_recv,
        rs_send2, rs_recv2, ag_send2, ag_recv2, x1s, x1r, x2s, x2r, zs, zr, as_, ar,
        cs, cr, y2s, y2r, y1s, y1r, hs, hr, gps, gpr, gs, gr, act_sem,
    ) = refs[48:]
    p, s = lax.axis_index("feat"), lax.axis_index("seq")
    x, z = p // 2, p % 2
    side, back, up = 2 * (x + 1 - 2 * (x % 2)) + z, 2 * (3 - x) + z, 2 * x + 1 - z
    core, y, half = s % 2, (s // 2) % 4, s // 8
    slab, rank = part.shape[1], part.shape[2]
    small, width = tokv.shape[2], tokv.shape[3]
    rows = FEATS * slab
    mid_rows = rows // 2
    blocks = width // BLK
    row_blocks = wv.shape[0] // BLK
    wide = LEVELS * BLK
    piece = crecv.shape[1]

    def part_of(ref, h, c):
        return ref.at[pl.ds(h * mid_rows + c * small, small), :]

    tok_loads = [pltpu.make_async_copy(tok.at[:, h], tokv.at[h], lsem.at[h]) for h in range(2)]
    loads = [pltpu.make_async_copy(w_hbm, wv, lsem.at[2]), pltpu.make_async_copy(left_hbm, leftv, lsem.at[3])]
    for h in range(2):
        for c in range(FEATS):
            loads.append(
                pltpu.make_async_copy(cot_hbm.at[c, h], part_of(gp, h, c), lsem.at[4 + h * FEATS + c])
            )
    for copy in tok_loads + loads:
        copy.start()
    greet([((p + k) % FEATS, s) for k in range(1, FEATS)] + [(p, (s + k) % SEQS) for k in range(1, SEQS)])

    def chunk(pair, c):
        return pair[c // 4].at[pl.ds((c % 4) * 2, 2)]

    def own_chunk(c):
        return tok.at[pl.ds((c % 4) * 2, 2), c // 4]

    def at(ref, c):
        return ref.at[pl.ds(c * slab, slab), :]

    own = [remote(own_chunk(c), chunk((x2a, x2b), c), x_send.at[c], x_recv.at[c], side, s) for c in range(FEATS)]
    passed = [
        remote(chunk((x2a, x2b), c), chunk((x1a, x1b), c), f_send.at[c], f_recv.at[c], back, s) for c in range(FEATS)
    ]
    across = [remote(own_chunk(c), chunk((x3a, x3b), c), z_send.at[c], z_recv.at[c], up, s) for c in range(FEATS)]
    latent = FeatSum(p, s, part, outgoing, landed, shared, (rs_send, rs_recv, ag_send, ag_recv))
    own[0].start()
    across[0].start()
    for copy in tok_loads:
        copy.wait()
    for c in range(FEATS):
        mine = tokv[c // 4, (c % 4) * 2 : (c % 4) * 2 + 2].reshape(slab, width)
        part[c] = jnp.dot(mine, right[...], preferred_element_type=F32)
    latent.send()
    for c in (1,):
        own[c].start()
        across[c].start()

    sums[0] = jnp.zeros(sums.shape[1:], F32)

    def relay(c):
        own[c].wait_recv()
        passed[c].start()
        if c + 2 < FEATS:
            own[c + 2].start()
            across[c + 2].start()

    relay(0)
    latent.share()
    for c in range(1, 5):
        relay(c)

    def halves(h):
        return slice(h * mid_rows, (h + 1) * mid_rows)

    def repack(h):
        for j, source in enumerate((tokv.at[h], (x1a, x1b)[h], (x2a, x2b)[h], (x3a, x3b)[h])):
            for b in range(blocks):
                block = source[:, :, b * BLK : (b + 1) * BLK].reshape(mid_rows, BLK)
                xall[b, halves(h), j * BLK : (j + 1) * BLK] = block

    def picked(here, f):
        return jnp.concatenate([xall[links[row_blocks + blocks + f], here, :], lat[here, :]], axis=1)

    curve = math.sqrt(2.0 / math.pi)

    def forward(h, first, count):
        here = slice(h * mid_rows, (h + 1) * mid_rows)

        def one(f):
            fr = block_of(f)
            wl = jnp.concatenate([wv[fr, :], leftv[fr, :]], axis=1)
            pre = lax.dot_general(picked(halves(h), f), wl, (((1,), (1,)), ((), ())), preferred_element_type=F32)
            square = pre * pre
            th = jnp.tanh(curve * (pre + 0.044715 * (square * pre)))
            cdf = 0.5 + 0.5 * th
            actv[here, fr] = (pre * cdf).astype(BF16)
            slope = cdf + (0.5 * curve) * pre * (1.0 - th * th) * (1.0 + (3.0 * 0.044715) * square)
            gp[here, fr] = (gp[here, fr].astype(F32) * slope).astype(BF16)

        loop(first, count, one)

    def spread(h, begin, count):
        here = slice(h * mid_rows, (h + 1) * mid_rows)

        def one(f):
            fr = block_of(f)
            sums[f + 1] = sums[links[f]] + jnp.dot(gp[here, fr], wv[fr, :], preferred_element_type=F32)

        loop(begin, count, one)

    def collect(h):
        here = slice(h * mid_rows, (h + 1) * mid_rows)
        for b in range(blocks):
            total = sums[links[row_blocks + b]].astype(BF16)
            for j in range(LEVELS):
                terms[j, here, b * BLK : (b + 1) * BLK] = total[:, j * BLK : (j + 1) * BLK]

    first = [remote(at(terms.at[1], c), at(rx1, c), x1s.at[c], x1r.at[c], back, s) for c in range(FEATS)]
    second = [remote(at(rx1, c), at(rx2, c), x2s.at[c], x2r.at[c], side, s) for c in range(FEATS)]
    upward = [remote(at(terms.at[3], c), at(rz, c), zs.at[c], zr.at[c], up, s) for c in range(FEATS)]

    def send_terms(c):
        first[c].start()
        upward[c].start()

    def hand_on(c):
        here = slice(c * slab, (c + 1) * slab)
        first[c].wait_recv()
        rx1[here, :] = (terms[2, here, :].astype(F32) + rx1[here, :].astype(F32)).astype(BF16)
        second[c].start()

    def back_sum_of(h):
        return FeatSum(
            p, s, backp.at[h], backo.at[h], backl.at[h], backs.at[h],
            (rs_send2.at[h], rs_recv2.at[h], ag_send2.at[h], ag_recv2.at[h]),
        )

    back_sums = [back_sum_of(0), back_sum_of(1)]

    def start_back(h):
        for c in range(FEATS):
            here = slice(h * mid_rows + c * small, h * mid_rows + (c + 1) * small)
            if c % 4 == 0:
                wider = slice(h * mid_rows + c * small, h * mid_rows + (c + 4) * small)
                four = jnp.dot(gp[wider, :], leftv[...], preferred_element_type=F32)
            backp[h, c] = four[(c % 4) * small : (c % 4 + 1) * small, :]
        back_sums[h].send()

    def end_back(h):
        back_sums[h].finish()
        for c in range(FEATS):
            backv[h * mid_rows + c * small : h * mid_rows + (c + 1) * small, :] = backs[h, c]

    regroup = []
    for h in range(2):
        for k in range(1, FEATS):
            there = (p + k) % FEATS
            src = terms.at[0, pl.ds(pl.multiple_of(h * mid_rows + there * small, small), small), :]
            dst = a2a.at[p, pl.ds(h * small, small), :]
            regroup.append(remote(src, dst, as_.at[h, k - 1], ar.at[h, k - 1], there, s))

    def finish_half(h):
        lows = lax.dot_general(
            backv[halves(h), :], right[...], (((1,), (1,)), ((), ())), preferred_element_type=F32
        )
        for c in range(h * 4, h * 4 + 4):
            here = slice(c * slab, (c + 1) * slab)
            low = lows[(c % 4) * slab : (c % 4 + 1) * slab, :]
            second[c].wait_recv()
            upward[c].wait_recv()
            terms[0, here, :] = (
                low + terms[0, here, :].astype(F32) + rx2[here, :].astype(F32) + rz[here, :].astype(F32)
            ).astype(BF16)
        for copy in regroup[h * (FEATS - 1) : (h + 1) * (FEATS - 1)]:
            copy.start()
        a2a[p, h * small : (h + 1) * small, :] = terms[
            0, pl.ds(pl.multiple_of(h * mid_rows + p * small, small), small), :
        ]

    latent.finish()
    for c in range(FEATS):
        lat[c * slab : (c + 1) * slab, :] = shared[c]
    for c in range(4):
        passed[c].wait_recv()
        across[c].wait_recv()
    for copy in loads:
        copy.wait()
    repack(0)
    forward(0, 0, 12)
    relay(5)
    forward(0, 12, row_blocks - 12)
    relay(6)
    spread(0, 0, row_blocks // 2)
    relay(7)
    spread(0, row_blocks // 2, row_blocks - row_blocks // 2)
    collect(0)
    start_back(0)
    send_terms(0)
    send_terms(1)
    for c in range(4, FEATS):
        passed[c].wait_recv()
        across[c].wait_recv()
    repack(1)
    forward(1, 0, 12)
    hand_on(0)
    send_terms(2)
    back_sums[0].share()
    forward(1, 12, row_blocks - 12)
    hand_on(1)
    send_terms(3)
    act_outs = []
    for h in range(2):
        for c in range(FEATS):
            act_outs.append(
                pltpu.make_async_copy(part_of(actv, h, c), act_hbm.at[c, h], act_sem.at[h * FEATS + c])
            )
            act_outs[-1].start()

    def seq_at(half_, y_, core_):
        return half_ * 8 + y_ * 2 + core_

    def grad_rows(first_block, count):
        def one(f):
            fr = block_of(f)
            xl = picked(slice(0, rows), f)
            grads[fr, :] = (
                lax.dot_general(gp[:, fr], xl, (((0,), (0,)), ((), ())), preferred_element_type=F32) * norm_scale
            ).astype(BF16)

        loop(first_block, count, one)

    slots = [(dy, h) for dy in (2, 1, 3, 0) for h in (0, 1)]

    def rows_of(dy, h, core_):
        there = half if h == 1 else 1 - half
        return pl.ds(pl.multiple_of(seq_at(there, (y + dy) % 4, core_) * piece, 32), piece)

    sibling = seq_at(half, y, 1 - core)
    up_y, down_y = seq_at(half, (y + 1) % 4, core), seq_at(half, (y + 3) % 4, core)
    other_half = seq_at(1 - half, y, core)
    cores = [
        remote(grads.at[rows_of(dy, h, 1 - core), :], crecv.at[i], cs.at[i], cr.at[i], p, sibling)
        for i, (dy, h) in enumerate(slots)
    ]
    far = [
        remote(q.at[0], ry2.at[0], y2s.at[0], y2r.at[0], p, up_y),
        remote(q.at[1], ry2.at[1], y2s.at[1], y2r.at[1], p, down_y),
    ]
    near = [remote(q.at[2 + i], ry1.at[i], y1s.at[i], y1r.at[i], p, up_y if i < 2 else down_y) for i in range(4)]

    def pair_sum(i, *others):
        dy, h = slots[i]
        total = grads[rows_of(dy, h, core), :].astype(F32) + crecv[i].astype(F32)
        for other in others:
            total = total + other[...].astype(F32)
        return total

    def send_sum(i, copy, *others):
        cores[i].wait_recv()
        q[i] = pair_sum(i, *others).astype(BF16)
        copy.start()

    far_pair = ((y + 2) % 4) // 2
    per_pair = row_blocks // 4
    spread(1, 0, row_blocks)
    collect(1)
    hand_on(2)
    send_terms(4)
    send_terms(5)
    start_back(1)
    for h in (0, 1):
        grad_rows(far_pair * per_pair + h * 2 * per_pair, per_pair)
    cores[0].start()
    cores[1].start()
    hand_on(3)
    for h in (0, 1):
        grad_rows((1 - far_pair) * per_pair + h * 2 * per_pair, per_pair)
    for i in (4, 2, 3, 5, 6, 7):
        cores[i].start()
    for i in range(2):
        send_sum(i, far[i])
    end_back(0)
    finish_half(0)
    send_sum(4, near[2])
    hand_on(4)
    send_terms(6)
    back_sums[1].share()
    hand_on(5)
    send_terms(7)
    far[0].wait_recv()
    send_sum(2, near[0], ry2.at[0])
    send_sum(3, near[1])
    far[1].wait_recv()
    send_sum(5, near[3], ry2.at[1])
    hand_on(6)
    end_back(1)
    product = (
        lax.dot_general(
            tokv[...].reshape(rows, width), backv[...], (((0,), (0,)), ((), ())), preferred_element_type=F32
        )
        * norm_scale
    )
    grow = gright.shape[0]
    for k in range(SEQS):
        grsend[k // 2, k % 2] = product[k * grow : (k + 1) * grow, :].astype(BF16)
    pair = remote(grsend.at[:, 1 - core], grpair, gps, gpr, p, sibling)
    pair.start()
    place_ = half * 4 + y
    rights = []
    for k in range(1, SEQS // 2):
        there = (place_ + k) % (SEQS // 2)
        rights.append(
            remote(grsum.at[there], grrecv.at[k - 1], gs.at[k - 1], gr.at[k - 1], p, there * 2 + core)
        )
    hand_on(7)
    pair.wait_recv()
    grsum[...] = (grsend[:, core].astype(F32) + grpair[...].astype(F32)).astype(BF16)
    for copy in rights:
        copy.start()
    finish_half(1)
    for copy in (near[0], near[2], cores[6]):
        copy.wait_recv()
    zsend[...] = pair_sum(6, ry1.at[0], ry1.at[2]).astype(BF16)
    cross = remote(zsend, zrecv, hs, hr, p, other_half)
    cross.start()
    for copy in (near[1], near[3], cores[7]):
        copy.wait_recv()
    total = grsend[place_, core].astype(F32) + grpair[place_].astype(F32)
    for k, copy in enumerate(rights):
        copy.wait_recv()
        total = total + grrecv[k].astype(F32)
    gright[...] = total
    cross.wait_recv()
    grad[...] = pair_sum(7, ry1.at[1], ry1.at[3], zrecv)
    for copy in regroup:
        copy.wait_recv()
    latent.drain()
    for each in back_sums:
        each.drain()
    for copy in own + passed + across + first + second + upward + cores + far + near + rights + regroup + [cross, pair]:
        copy.wait_send()
    for copy in act_outs:
        copy.wait()


def chain_links(pattern, blocks):
    count = pattern.shape[0]
    total = 2 * count + blocks
    place = lax.rem(pattern[:, 0], blocks)
    r = lax.broadcasted_iota(jnp.int32, (total, count), 0)
    g = lax.broadcasted_iota(jnp.int32, (total, count), 1)
    across = jnp.broadcast_to(place[None, :], (total, count))
    down = jnp.broadcast_to(jnp.pad(place, (0, total - count))[:, None], (total, count))
    is_row, is_place = r < count, r < count + blocks
    linked = jnp.where(is_row, (down == across) & (g < r), across == r - count)
    found = jnp.where(linked, g + 1, 0)
    own = jnp.where(g == r - count - blocks, across, 0)
    return jnp.max(jnp.where(is_place, found, own), axis=1)


def fused(tokens, weights, left, right, pattern, cotangent, norm_scale):
    rows, width = tokens.shape
    out_rows, wide = weights.shape
    rank = left.shape[1]
    slab = rows // FEATS
    row_blocks, blocks = out_rows // BLK, width // BLK
    piece, grow = out_rows // SEQS, width // SEQS
    all_wide = wide + rank
    any_spec = pl.BlockSpec(memory_space=pl.ANY)
    vmem_spec = pl.BlockSpec(memory_space=pltpu.VMEM)
    smem_spec = pl.BlockSpec(memory_space=pltpu.SMEM)
    dma = pltpu.SemaphoreType.DMA
    d8, d7, d4, d2, d27 = dma((8,)), dma((7,)), dma((4,)), dma((2,)), dma((2, 7))
    small = slab // 2
    half = pltpu.VMEM((FEATS, small, width), BF16)
    whole = pltpu.VMEM((rows, width), BF16)
    slabs, slabs7 = pltpu.VMEM((FEATS, slab, rank), BF16), pltpu.VMEM((FEATS - 1, slab, rank), BF16)
    flat = pltpu.VMEM((rows, rank), BF16)
    return pl.pallas_call(
        functools.partial(kernel, norm_scale),
        out_shape=(
            jax.ShapeDtypeStruct((FEATS, 2, slab // 2, out_rows), BF16),
            jax.ShapeDtypeStruct((FEATS, slab, width), BF16),
            jax.ShapeDtypeStruct((piece, all_wide), F32),
            jax.ShapeDtypeStruct((grow, rank), F32),
        ),
        in_specs=[smem_spec, any_spec, any_spec, any_spec, any_spec, vmem_spec],
        out_specs=(any_spec, vmem_spec, vmem_spec, vmem_spec),
        scratch_shapes=[
            pltpu.VMEM((blocks, rows, wide), BF16),
            pltpu.VMEM((2, FEATS, small, width), BF16), half, half, half, half, half, half,
            pltpu.VMEM((out_rows, wide), BF16), pltpu.VMEM((out_rows, rank), BF16),
            pltpu.VMEM((rows, out_rows), BF16), pltpu.VMEM((rows, out_rows), BF16),
            pltpu.VMEM((row_blocks + 1, rows // 2, wide), F32),
            pltpu.VMEM((LEVELS, rows, width), BF16),
            pltpu.VMEM((out_rows, all_wide), BF16),
            pltpu.VMEM((FEATS, slab, rank), F32), slabs, slabs7, slabs, flat,
            pltpu.VMEM((2, FEATS, small, rank), F32), pltpu.VMEM((2, FEATS, small, rank), BF16),
            pltpu.VMEM((2, FEATS - 1, small, rank), BF16), pltpu.VMEM((2, FEATS, small, rank), BF16), flat,
            whole, whole, whole,
            pltpu.VMEM((8, piece, all_wide), BF16), pltpu.VMEM((6, piece, all_wide), BF16),
            pltpu.VMEM((2, piece, all_wide), BF16), pltpu.VMEM((4, piece, all_wide), BF16),
            pltpu.VMEM((piece, all_wide), BF16), pltpu.VMEM((piece, all_wide), BF16),
            pltpu.VMEM((SEQS // 2, 2, grow, rank), BF16), pltpu.VMEM((SEQS // 2, grow, rank), BF16),
            pltpu.VMEM((SEQS // 2, grow, rank), BF16), pltpu.VMEM((SEQS // 2 - 1, grow, rank), BF16),
            dma((20,)), d8, d8, d8, d8, d8, d8, d7, d7, d7, d7, d27, d27, d27, d27,
            d8, d8, d8, d8, d8, d8, d27, d27, d8, d8, d2, d2, d4, d4, dma, dma, dma, dma, d7, d7, dma((16,)),
        ],
        compiler_params=pltpu.CompilerParams(collective_id=0, has_side_effects=True, vmem_limit_bytes=VMEM_LIMIT),
    )(
        chain_links(pattern, blocks),
        tokens.reshape(FEATS, 2, slab // 2, width),
        weights,
        left,
        cotangent.reshape(FEATS, 2, slab // 2, out_rows),
        right,
    )


def place_kernel(wide, act, a2a, grad, gright, act_o, gin_o, gb_o, gl_o, gr_o, actv, a2av, gradv, grv, in_sem, out_sem):
    parts = 8
    step = act.shape[0] // parts
    width = a2a.shape[2]
    rows = [pl.ds(i * step, step) for i in range(parts)]
    moves = [(act.at[r, :], actv.at[r, :], [(actv.at[r, :], act_o.at[r, :])]) for r in rows]
    moves.append(
        (grad, gradv, [(gradv.at[:, pl.ds(0, wide)], gb_o), (gradv.at[:, pl.ds(wide, gradv.shape[1] - wide)], gl_o)])
    )
    moves.append((gright, grv, [(grv, gr_o)]))
    moves += [
        (a2a.at[c], a2av.at[c], [(a2av.at[c], gin_o.at[:, pl.ds(c * width, width)])]) for c in range(a2a.shape[0])
    ]
    ins = [pltpu.make_async_copy(src, mid, in_sem.at[i]) for i, (src, mid, _) in enumerate(moves)]
    for copy in ins:
        copy.start()
    outs = []
    for copy, (_, _, after) in zip(ins, moves):
        copy.wait()
        for src, dst in after:
            outs.append(pltpu.make_async_copy(src, dst, out_sem.at[len(outs)]))
            outs[-1].start()
    for copy in outs:
        copy.wait()


def place(act, a2a, grad, gright, wide):
    any_spec = pl.BlockSpec(memory_space=pl.ANY)
    feats, slab, width = a2a.shape
    piece, all_wide = grad.shape
    dma = pltpu.SemaphoreType.DMA
    return pl.pallas_call(
        functools.partial(place_kernel, wide),
        out_shape=(
            jax.ShapeDtypeStruct(act.shape, BF16),
            jax.ShapeDtypeStruct((slab, feats * width), BF16),
            jax.ShapeDtypeStruct((piece, wide), F32),
            jax.ShapeDtypeStruct((piece, all_wide - wide), F32),
            jax.ShapeDtypeStruct(gright.shape, F32),
        ),
        in_specs=[any_spec] * 4,
        out_specs=(any_spec,) * 5,
        scratch_shapes=[
            pltpu.VMEM(act.shape, BF16), pltpu.VMEM(a2a.shape, BF16),
            pltpu.VMEM(grad.shape, F32), pltpu.VMEM(gright.shape, F32),
            dma((18,)), dma((19,)),
        ],
        compiler_params=pltpu.CompilerParams(vmem_limit_bytes=VMEM_LIMIT),
    )(act, a2a, grad, gright)


def local(tokens, block_weights, left_factor, right_factor, pattern, cotangent):
    norm_scale = 1.0 / math.sqrt(tokens.shape[0] * lax.axis_size("seq"))
    act, a2a, grad, gright = fused(
        tokens, block_weights, left_factor, right_factor, pattern, cotangent, norm_scale
    )
    activated, grad_input, grad_blocks, grad_left, grad_right = place(
        act.reshape(cotangent.shape), a2a, grad, gright, block_weights.shape[1]
    )
    return activated, grad_input[None], grad_blocks, grad_left, grad_right


def solution(mesh):
    in_specs = (
        P("seq", "feat"),
        P("feat", None),
        P("feat", None),
        P("feat", None),
        P("feat", None),
        P("seq", "feat"),
    )
    out_specs = (
        P("seq", "feat"),
        P("seq", "feat", None),
        P(("feat", "seq"), None),
        P(("feat", "seq"), None),
        P(("feat", "seq"), None),
    )
    return jax.shard_map(local, mesh=mesh, in_specs=in_specs, out_specs=out_specs, check_vma=False)
```
